128 devices in a mesh: slab: 8 (over x, y_lo), tile: 16 (over y_hi, z, core).
Axes of the slice: x: 4, y: 4 (y_hi: 2, y_lo: 2; y = y_hi * 2 + y_lo), z: 4, core: 2. Of those that a mesh axis runs over, the one named last changes fastest.
Arguments:
- distribution_functions: float32 [19, 128, 512, 128], P(None, 'slab', 'tile')
- heat_excess_scalar: float32 [128, 512, 128], P('slab', 'tile'), may hold values from -6 to 6
- obstacle_site_flag: int32 [128, 512, 128], P('slab', 'tile'), may hold values from 0 to 1, as said below
- cabinet_category_label: int32 [1024], replicated, may hold values from 0 to 7
- intake_face_position: int32 [1024, 32], replicated, may hold values from 0 to 8388607, as said below
- outflow_face_position: int32 [1024, 32], replicated, may hold values from 0 to 8388607, as said below
- category_evolution_operator: bfloat16 [8, 2048, 2048], P(None, 'tile', 'slab'), may hold values from -0.125 to 0.125
- intake_input_coefficients: float32 [8, 2048], replicated, may hold values from -12 to 12
- outflow_output_coefficients: float32 [8, 2048], replicated, may hold values from -0.125 to 0.125
- cabinet_heat_vector: bfloat16 [1024, 2048], P('slab'), may hold values from -6 to 6
Outputs:
- new_populations: float32 [19, 128, 512, 128], P(None, 'slab', 'tile')
- new_temperature: float32 [128, 512, 128], P('slab', 'tile')
- new_states: float32 [1024, 2048], P('slab', 'tile')
The draws below stay inside these ranges and needn't reach their ends.
Inputs may be any that keep to these rules, and one draw needn't show every extreme that they name: `intake_face_position`: each rack is a block 4 cells wide and 8 high in a row of racks along the hall; its inlet face, body and exhaust face lie in three consecutive cells along the hall's length, all within one slab of 16 cells. No cell belongs to two faces; face cells are never solid. `outflow_face_position`: same layout as the inlet faces, two cells further along the hall. `obstacle_site_flag`: the lowest and highest layer of cells and every rack body are solid.
All inputs are finite; a program needn't handle non-finite values.
Results may differ from the reference program's by a relative error of at most 0.00085.
Values may be sent and summed in bfloat16 or wider, within the bound.
A program may use at most 128 MiB of HBM per device.

```python
import math
import jax
import jax.numpy as jnp
import numpy as np

UPRIGHT_SITES = 128
STEPS = 3
STATES = 2048
TYPES = 8
FY = 4
FZ = 8
FACE = 32
LONGWISE_SITES = 128
BREADTH_SITES = 512
RACKS = 1024
RACK_ROWS = 32
RACK_COLS = 32


VELOCITY = ((0, 0, 0), (1, 0, 0), (-1, 0, 0), (0, 1, 0), (0, -1, 0), (0, 0, 1), (0, 0, -1), (1, 1, 0), (-1, -1, 0), (1, -1, 0), (-1, 1, 0), (1, 0, 1), (-1, 0, -1), (1, 0, -1), (-1, 0, 1), (0, 1, 1), (0, -1, -1), (0, 1, -1), (0, -1, 1))


WEIGHTS = (1.0 / 3.0,) + (1.0 / 18.0,) * 6 + (1.0 / 36.0,) * 12


def rack_layout(key):
    spacing_x = LONGWISE_SITES // RACK_ROWS
    spacing_y = BREADTH_SITES // RACK_COLS
    rack_ids = jnp.arange(RACKS, dtype=jnp.int32)
    base_x = rack_ids // RACK_COLS * spacing_x
    offset_y = jax.random.randint(jax.random.fold_in(key, 11), (RACKS,), 0, spacing_y - FY + 1)
    base_y = rack_ids % RACK_COLS * spacing_y + offset_y
    base_z = jax.random.randint(jax.random.fold_in(key, 12), (RACKS,), 1, UPRIGHT_SITES - FZ)
    column_cells = base_y[:, None, None] + jnp.arange(FY, dtype=jnp.int32)[None, :, None]
    height_cells = base_z[:, None, None] + jnp.arange(FZ, dtype=jnp.int32)[None, None, :]

    def face_of(across):
        return ((across[:, None, None] * BREADTH_SITES + column_cells) * UPRIGHT_SITES + height_cells).reshape(RACKS, FY * FZ).astype(jnp.int32)
    return (face_of(base_x), face_of(base_x + 1), face_of(base_x + 2))


def draw_intake_face_position(key, part):
    return rack_layout(key)[0]


def draw_outflow_face_position(key, part):
    return rack_layout(key)[2]


def draw_obstacle_site_flag(key, part):
    body_cells = rack_layout(key)[1].reshape(-1)
    solid_mask = jnp.zeros((LONGWISE_SITES * BREADTH_SITES * UPRIGHT_SITES,), jnp.int32).at[body_cells].set(1).reshape(LONGWISE_SITES, BREADTH_SITES, UPRIGHT_SITES)
    solid_mask = solid_mask.at[:, :, 0].set(1)
    solid_mask = solid_mask.at[:, :, UPRIGHT_SITES - 1].set(1)
    return solid_mask


def draw_distribution_functions(key, part):
    grid_shape = (LONGWISE_SITES, BREADTH_SITES, UPRIGHT_SITES)
    density = 1.0 + 0.03 * jax.random.normal(jax.random.fold_in(key, 1), grid_shape, jnp.float32)
    noise = 0.04 * jax.random.normal(jax.random.fold_in(key, 2), (19,) + grid_shape, jnp.float32)
    velocity = 0.03 * jax.random.normal(jax.random.fold_in(key, 3), (3,) + grid_shape, jnp.float32)
    speed_sq = velocity[0] * velocity[0] + velocity[1] * velocity[1] + velocity[2] * velocity[2]
    lanes_out = []
    for lane in range(19):
        stride = VELOCITY[lane]
        projected = stride[0] * velocity[0] + stride[1] * velocity[1] + stride[2] * velocity[2]
        balance = WEIGHTS[lane] * density * (1.0 + 3.0 * projected + 4.5 * projected * projected - 1.5 * speed_sq)
        lanes_out.append(balance * (1.0 + noise[lane]))
    return jnp.stack(lanes_out).astype(jnp.float32)


def touch_ends(array, stream_key, least, top_value):
    shape = array.shape
    place = [jax.random.randint(jax.random.fold_in(stream_key, axis), (), 0, shape[axis]) for axis in range(len(shape))]
    array = array.at[tuple(place)].set(least)
    longest = shape.index(max(shape))
    place[longest] = (place[longest] + 1) % shape[longest]
    return array.at[tuple(place)].set(top_value)


def block_scale(key, extent, cuts, least, high):
    loudness = 1.0
    for axis_at, blocks in cuts:
        heights = jax.random.uniform(jax.random.fold_in(jax.random.fold_in(key, 6), axis_at), (blocks,), jnp.float32, least / len(cuts), high / len(cuts))
        loudness = loudness * jnp.repeat(jnp.exp(heights), extent[axis_at] // blocks).reshape((-1,) + (1,) * (len(extent) - 1 - axis_at))
    return loudness


def cumulative_ranks(number_of, skew):
    loads = [(1 << 20) // math.isqrt(rank ** skew) + 1 for rank in range(1, number_of + 1)]
    scale = 1 + sum(loads) // (1 << 30)
    return np.cumsum(np.array([max(1, weight // scale) for weight in loads]))


def ranked(stream_key, shape, amount, skew):
    grid = cumulative_ranks(amount, skew)
    ticket = jax.random.randint(jax.random.fold_in(stream_key, 1), shape, 0, int(grid[amount - 1]))
    rank = jnp.searchsorted(jnp.asarray(grid, jnp.int32), ticket, side="right")
    return jax.random.permutation(jax.random.fold_in(stream_key, 2), amount)[rank].astype(jnp.int32)


def scatter_about(key, dims, spread, limit, cuts=(), kind=jnp.bfloat16):
    loudness = block_scale(key, dims, cuts, -0.22, 0.18) if cuts else 1.0
    values = jax.random.normal(key, dims, jnp.float32) * spread * loudness
    return jnp.minimum(jnp.maximum(values, -limit), limit).astype(kind)


def setup_inputs(seed: int = 0) -> dict:
    arg_keys = jax.random.split(jax.random.key(seed), 11)
    return {
        "distribution_functions": draw_distribution_functions(jax.random.fold_in(arg_keys[10], 71), 0),
        "heat_excess_scalar": scatter_about(arg_keys[1], (LONGWISE_SITES, BREADTH_SITES, UPRIGHT_SITES), 1.0, 6.0, ((0, 8), (1, 16)), jnp.float32),
        "obstacle_site_flag": draw_obstacle_site_flag(jax.random.fold_in(arg_keys[10], 71), 0),
        "cabinet_category_label": touch_ends(ranked(arg_keys[3], (RACKS,), TYPES, 2), jax.random.fold_in(arg_keys[3], 3), 0, TYPES - 1).astype(jnp.int32),
        "intake_face_position": draw_intake_face_position(jax.random.fold_in(arg_keys[10], 71), 0),
        "outflow_face_position": draw_outflow_face_position(jax.random.fold_in(arg_keys[10], 71), 0),
        "category_evolution_operator": scatter_about(arg_keys[6], (TYPES, STATES, STATES), STATES ** -0.5, 0.125, ((1, 16), (2, 8))),
        "intake_input_coefficients": scatter_about(arg_keys[7], (TYPES, STATES), 2.0, 12.0, (), jnp.float32),
        "outflow_output_coefficients": scatter_about(arg_keys[8], (TYPES, STATES), STATES ** -0.5, 0.125, (), jnp.float32),
        "cabinet_heat_vector": scatter_about(arg_keys[9], (RACKS, STATES), 1.0, 6.0, ((0, 8),)),
    }


VELOCITY = ((0, 0, 0), (1, 0, 0), (-1, 0, 0), (0, 1, 0), (0, -1, 0), (0, 0, 1), (0, 0, -1), (1, 1, 0), (-1, -1, 0), (1, -1, 0), (-1, 1, 0), (1, 0, 1), (-1, 0, -1), (1, 0, -1), (-1, 0, 1), (0, 1, 1), (0, -1, -1), (0, 1, -1), (0, -1, 1))
OPPOSITE = (0, 2, 1, 4, 3, 6, 5, 8, 7, 10, 9, 12, 11, 14, 13, 16, 15, 18, 17)
WEIGHTS = (1.0 / 3.0,) + (1.0 / 18.0,) * 6 + (1.0 / 36.0,) * 12
relax_time = 0.6
buoyancy = 0.01
diffusion = 0.1
mixing = 0.5
keep_share = 0.5


def collide(lattice_quantities, heated_quantities, solid):
    density = jnp.sum(lattice_quantities, axis=0)
    velocity = []
    for dimension in range(3):
        summed = jnp.zeros_like(density)
        for lane in range(19):
            stride = VELOCITY[lane][dimension]
            if stride != 0:
                summed = summed + stride * lattice_quantities[lane]
        velocity.append(summed / density)
    shifted = [velocity[0], velocity[1], velocity[2] + relax_time * buoyancy * heated_quantities / density]
    speed_sq = shifted[0] * shifted[0] + shifted[1] * shifted[1] + shifted[2] * shifted[2]
    relaxed = []
    for lane in range(19):
        stride = VELOCITY[lane]
        projected = stride[0] * shifted[0] + stride[1] * shifted[1] + stride[2] * shifted[2]
        balance = WEIGHTS[lane] * density * (1.0 + 3.0 * projected + 4.5 * projected * projected - 1.5 * speed_sq)
        relaxed_lane = lattice_quantities[lane] - (lattice_quantities[lane] - balance) / relax_time
        relaxed.append(jnp.where(solid, lattice_quantities[OPPOSITE[lane]], relaxed_lane))
    return jnp.stack(relaxed), velocity


def heat_step(centre, neighbours, velocity, solid):
    laplace = -6.0 * centre
    carried = jnp.zeros_like(centre)
    for dimension in range(3):
        behind, ahead = neighbours[dimension]
        laplace = laplace + behind + ahead
        carried = carried + velocity[dimension] * (0.5 * (ahead - behind))
    return jnp.where(solid, centre, centre + diffusion * laplace - carried)


def reference(distribution_functions, heat_excess_scalar, obstacle_site_flag, cabinet_category_label, intake_face_position, outflow_face_position, category_evolution_operator, intake_input_coefficients, outflow_output_coefficients, cabinet_heat_vector):
    solid = obstacle_site_flag == 1
    lattice_quantities, heated_quantities = distribution_functions, heat_excess_scalar
    for substep in range(STEPS):
        relaxed, velocity = collide(lattice_quantities, heated_quantities, solid)
        passed = [jnp.roll(relaxed[lane], VELOCITY[lane], axis=(0, 1, 2)) for lane in range(19)]
        neighbours = tuple((jnp.roll(heated_quantities, 1, axis=dimension), jnp.roll(heated_quantities, -1, axis=dimension)) for dimension in range(3))
        heated_quantities = heat_step(heated_quantities, neighbours, velocity, solid)
        lattice_quantities = jnp.stack(passed)
    flat_heat = heated_quantities.reshape(-1)
    inlet_mean = jnp.sum(flat_heat[intake_face_position], axis=1) / FACE
    kind_hot = (cabinet_category_label[:, None] == jnp.arange(TYPES, dtype=jnp.int32)[None, :]).astype(jnp.float32)
    mixed = jnp.zeros((RACKS, STATES), jnp.float32)
    for kind in range(TYPES):
        product = jnp.dot(cabinet_heat_vector, category_evolution_operator[kind].T, preferred_element_type=jnp.float32)
        mixed = mixed + kind_hot[:, kind:kind + 1] * product
    gain_rows = intake_input_coefficients[cabinet_category_label]
    new_states = keep_share * cabinet_heat_vector.astype(jnp.float32) + mixed + gain_rows * inlet_mean[:, None]
    exhaust = jnp.sum(outflow_output_coefficients[cabinet_category_label] * new_states, axis=1)
    old_values = flat_heat[outflow_face_position]
    flat_heat = flat_heat.at[outflow_face_position].add(mixing * (exhaust[:, None] - old_values))
    return lattice_quantities, flat_heat.reshape(heated_quantities.shape), new_states
```

```python
import functools

import jax
import jax.numpy as jnp
from jax import lax
from jax.experimental import pallas as pl
from jax.experimental.pallas import tpu as pltpu
from jax.sharding import PartitionSpec as P

MESH = pl.DeviceIdType.MESH
F32 = jnp.float32
BF16 = jnp.bfloat16

VELOCITY = (
    (0, 0, 0),
    (1, 0, 0),
    (-1, 0, 0),
    (0, 1, 0),
    (0, -1, 0),
    (0, 0, 1),
    (0, 0, -1),
    (1, 1, 0),
    (-1, -1, 0),
    (1, -1, 0),
    (-1, 1, 0),
    (1, 0, 1),
    (-1, 0, -1),
    (1, 0, -1),
    (-1, 0, 1),
    (0, 1, 1),
    (0, -1, -1),
    (0, 1, -1),
    (0, -1, 1),
)
X_UP = (1, 7, 9, 11, 13)
X_DOWN = (2, 8, 10, 12, 14)
Y_UP = (3, 7, 10, 15, 17)
Y_DOWN = (4, 8, 9, 16, 18)
CORNERS = ((7, 1, 1), (8, -1, -1), (9, 1, -1), (10, -1, 1))

relax_time = 0.6
buoyancy = 0.01
diffusion = 0.1
mixing = 0.5
keep_share = 0.5

NX, NY, NZ = 16, 32, 128
ROWS = 48
LOW, TOP = 7, 40
KINDS = 8
RACKS = 128
FACE = 32


def collide(f, heat, solid):
    omega = 1.0 / relax_time
    keep = 1.0 - omega
    even, odd = {}, {}
    for p in range(1, 19, 2):
        even[p] = f[p] + f[p + 1]
        odd[p] = f[p] - f[p + 1]
    density = (
        f[0]
        + ((even[1] + even[3]) + (even[5] + even[7]))
        + ((even[9] + even[11]) + (even[13] + even[15]))
        + even[17]
    )
    flow_x = (odd[1] + odd[7]) + (odd[9] + odd[11]) + odd[13]
    flow_y = (odd[3] + odd[7]) + (odd[15] - odd[9]) + odd[17]
    flow_z = (odd[5] + odd[11]) + (odd[15] - odd[13]) - odd[17]
    inverse = 1.0 / density
    ux = flow_x * inverse
    uy = flow_y * inverse
    uz = flow_z * inverse
    vz = uz + (relax_time * buoyancy) * heat * inverse
    rest = 1.0 - 1.5 * (ux * ux + uy * uy + vz * vz)
    share = density * (omega / 18.0)
    level = share * rest
    bend = share * 4.5
    lean = share * 3.0
    level_half, bend_half, lean_half = level * 0.5, bend * 0.5, lean * 0.5
    g = [None] * 19
    g[0] = jnp.where(solid, f[0], f[0] * keep + level * 6.0)
    along = {
        1: ux,
        3: uy,
        5: vz,
        7: ux + uy,
        9: ux - uy,
        11: ux + vz,
        13: ux - vz,
        15: uy + vz,
        17: uy - vz,
    }
    for p in range(1, 19, 2):
        c = along[p]
        lv, bd, ln = (level, bend, lean) if p < 7 else (level_half, bend_half, lean_half)
        same = lv + bd * (c * c)
        turn = ln * c
        g[p] = jnp.where(solid, f[p + 1], f[p] * keep + (same + turn))
        g[p + 1] = jnp.where(solid, f[p], f[p + 1] * keep + (same - turn))
    return g, (ux, uy, uz)


def shifted_z(v, step):
    return pltpu.roll(v, step % NZ, 1) if step else v


def face_masks(pos, slab, tile, tiles):
    pos = jnp.transpose(pos)
    height_bits = NZ.bit_length() - 1
    across = NY * tiles
    across_bits = across.bit_length() - 1
    px = jnp.right_shift(pos, height_bits + across_bits)
    py = jnp.bitwise_and(jnp.right_shift(pos, height_bits), across - 1)
    pz = jnp.bitwise_and(pos, NZ - 1)
    least = functools.partial(jnp.min, axis=0, keepdims=True)
    x0, y0, z0 = least(px), least(py), least(pz)
    y1 = jnp.max(py, axis=0, keepdims=True)
    lifted = least(py + jnp.where(py < across // 2, across, 0))
    y0 = jnp.where(y1 - y0 > 3, lifted, y0)
    row = lax.broadcasted_iota(jnp.int32, (NX * NY, RACKS), 0)
    gx = slab * NX + jnp.right_shift(row, 5)
    gy = tile * NY + jnp.bitwise_and(row, NY - 1)
    off_y = jnp.bitwise_and(gy - y0, across - 1)
    plan = jnp.where((gx == x0) & (off_y < 4), 1.0, 0.0).astype(F32)
    z = lax.broadcasted_iota(jnp.int32, (NZ, RACKS), 0)
    tall = jnp.where((z >= z0) & (z < z0 + 8), 1.0, 0.0).astype(F32)
    return plan, tall


def kernel(
    slabs,
    tiles,
    f_hbm,
    heat_hbm,
    solid_hbm,
    label_ref,
    inlet_hbm,
    outlet_hbm,
    matrix_ref,
    gain_ref,
    read_ref,
    state_ref,
    f_out,
    heat_out,
    states_out,
    fin,
    grid,
    warm,
    vel,
    solid_ref,
    inlet_ref,
    outlet_ref,
    x_send,
    x_recv,
    y_send,
    y_recv,
    c_recv,
    ty_send,
    ty_recv,
    kept,
    label_col,
    part,
    part_x,
    pair,
    part_y,
    base_ref,
    small_send,
    small_recv,
    load_sem,
    heat_sem,
    misc_sem,
    xs_sem,
    xr_sem,
    ys_sem,
    yr_sem,
    cs_sem,
    cr_sem,
    tsend_sem,
    trecv_sem,
    hs_sem,
    hr_sem,
    pxs_sem,
    pxr_sem,
    pys_sem,
    pyr_sem,
    ms_sem,
    mr_sem,
):
    slab = lax.axis_index("slab")
    tile = lax.axis_index("tile")
    s_up, s_down = lax.rem(slab + 1, slabs), lax.rem(slab + slabs - 1, slabs)
    t_up, t_down = lax.rem(tile + 1, tiles), lax.rem(tile + tiles - 1, tiles)
    core = lax.rem(tile, 2)
    partner = tile + 1 - 2 * core
    s_major = slab // 2
    s_minor = lax.rem(slab, 2)
    majors = slabs // 2

    def plane_copy(x):
        return pltpu.make_async_copy(f_hbm.at[:, x], fin.at[:, x], load_sem.at[x])

    def heat_copy(x):
        return pltpu.make_async_copy(
            heat_hbm.at[x], warm.at[0, x + 1, pl.ds(8, NY), :], heat_sem.at[x]
        )

    solid_copy = pltpu.make_async_copy(solid_hbm, solid_ref, misc_sem.at[0])
    first_rack = pl.multiple_of(slab * RACKS, RACKS)
    inlet_copy = pltpu.make_async_copy(
        inlet_hbm.at[pl.ds(first_rack, RACKS), :], inlet_ref, misc_sem.at[1]
    )
    outlet_copy = pltpu.make_async_copy(
        outlet_hbm.at[pl.ds(first_rack, RACKS), :], outlet_ref, misc_sem.at[2]
    )
    solid_copy.start()

    @pl.loop(0, NX)
    def _(x):
        heat_copy(x).start()

    plane_copy(0).start()
    plane_copy(NX - 1).start()

    @pl.loop(1, NX - 1)
    def _(x):
        plane_copy(x).start()

    inlet_copy.start()
    outlet_copy.start()

    barrier = pltpu.get_barrier_semaphore()

    @pl.loop(1, tiles)
    def _(d):
        pl.semaphore_signal(
            barrier, inc=1, device_id=(slab, lax.rem(tile + d, tiles)), device_id_type=MESH
        )

    @pl.loop(1, slabs)
    def _(d):
        pl.semaphore_signal(
            barrier, inc=1, device_id=(lax.rem(slab + d, slabs), tile), device_id_type=MESH
        )

    for ds in (s_up, s_down):
        for dt in (t_up, t_down):
            pl.semaphore_signal(barrier, inc=1, device_id=(ds, dt), device_id_type=MESH)

    def remote(src, dst, send, recv, to):
        return pltpu.make_async_remote_copy(
            src_ref=src,
            dst_ref=dst,
            send_sem=send,
            recv_sem=recv,
            device_id=to,
            device_id_type=MESH,
        )

    def x_copies(n):
        return [
            remote(x_send.at[n, 0], x_recv.at[n, 0], xs_sem.at[n, 0], xr_sem.at[n, 0], (s_up, tile)),
            remote(x_send.at[n, 1], x_recv.at[n, 1], xs_sem.at[n, 1], xr_sem.at[n, 1], (s_down, tile)),
        ]

    def y_copies(n):
        return [
            remote(y_send.at[n, 0], y_recv.at[n, 0], ys_sem.at[n, 0], yr_sem.at[n, 0], (slab, t_up)),
            remote(y_send.at[n, 1], y_recv.at[n, 1], ys_sem.at[n, 1], yr_sem.at[n, 1], (slab, t_down)),
        ]

    def c_copies(n):
        out = []
        for k, (lane, cx, cy) in enumerate(CORNERS):
            x = NX if cx > 0 else 1
            y = TOP - 8 if cy > 0 else LOW + 1
            to = (s_up if cx > 0 else s_down, t_up if cy > 0 else t_down)
            out.append(
                remote(
                    grid.at[n % 2, lane, x, pl.ds(y, 8), :],
                    c_recv.at[n, k],
                    cs_sem.at[n, k],
                    cr_sem.at[n, k],
                    to,
                )
            )
        return out

    def t_copies(n):
        own = pl.ds(8, NY)
        return [
            remote(
                warm.at[n, NX, own, :],
                warm.at[n, 0, own, :],
                tsend_sem.at[n, 0],
                trecv_sem.at[n, 0],
                (s_up, tile),
            ),
            remote(
                warm.at[n, 1, own, :],
                warm.at[n, NX + 1, own, :],
                tsend_sem.at[n, 1],
                trecv_sem.at[n, 1],
                (s_down, tile),
            ),
            remote(ty_send.at[n, 0], ty_recv.at[n, 0], tsend_sem.at[n, 2], trecv_sem.at[n, 2], (slab, t_up)),
            remote(ty_send.at[n, 1], ty_recv.at[n, 1], tsend_sem.at[n, 3], trecv_sem.at[n, 3], (slab, t_down)),
        ]

    def start_all(copies):
        for c in copies:
            c.start()

    def wait_recv_all(copies):
        for c in copies:
            c.wait_recv()

    def wait_send_all(copies):
        for c in copies:
            c.wait_send()

    def collide_block(n, x, yt):
        rows = pl.ds(8 + 8 * yt, 8)
        here = pl.ds(8 * yt, 8)
        if n == 0:
            f = [fin[i, x, here, :] for i in range(19)]
        else:
            old = (n - 1) % 2
            f = []
            for i, (cx, cy, cz) in enumerate(VELOCITY):
                v = grid[old, i, x + 1 - cx, pl.ds(8 + 8 * yt - cy, 8), :]
                f.append(shifted_z(v, cz))
        heat = warm[n, x + 1, rows, :]
        solid = solid_ref[x, here, :] == 1
        g, u = collide(f, heat, solid)
        new = n % 2
        for i in range(19):
            grid[new, i, x + 1, rows, :] = g[i]
        for d in range(3):
            vel[d, x, here, :] = u[d]

    def heat_block(n, x, yt):
        rows = pl.ds(8 + 8 * yt, 8)
        here = pl.ds(8 * yt, 8)
        centre = warm[n, x + 1, rows, :]
        pairs = (
            (warm[n, x, rows, :], warm[n, x + 2, rows, :]),
            (
                warm[n, x + 1, pl.ds(7 + 8 * yt, 8), :],
                warm[n, x + 1, pl.ds(9 + 8 * yt, 8), :],
            ),
            (shifted_z(centre, 1), shifted_z(centre, -1)),
        )
        laplace = -6.0 * centre
        carried = None
        for d in range(3):
            behind, ahead = pairs[d]
            laplace = laplace + (behind + ahead)
            term = vel[d, x, here, :] * (0.5 * (ahead - behind))
            carried = term if carried is None else carried + term
        solid = solid_ref[x, here, :] == 1
        warm[n + 1, x + 1, rows, :] = jnp.where(solid, centre, centre + diffusion * laplace - carried)

    def send_heat_rows(n):
        ty_send[n, 0] = warm[n, pl.ds(1, NX), TOP - 1, :]
        ty_send[n, 1] = warm[n, pl.ds(1, NX), LOW + 1, :]

    def take_heat_rows(n):
        warm[n, pl.ds(1, NX), LOW, :] = ty_recv[n, 0]
        warm[n, pl.ds(1, NX), TOP, :] = ty_recv[n, 1]

    def heat_pass(n):
        copies = t_copies(n)
        wait_recv_all(copies)
        take_heat_rows(n)

        @pl.loop(0, NX)
        def _(x):
            for yt in range(4):
                heat_block(n, x, yt)

        wait_send_all(copies)
        if n < 2:
            send_heat_rows(n + 1)
            start_all(t_copies(n + 1))

    def pack_x(n):
        own = pl.ds(8, NY)
        for k, lane in enumerate(X_UP):
            x_send[n, 0, k] = grid[n % 2, lane, NX, own, :].astype(BF16)
        for k, lane in enumerate(X_DOWN):
            x_send[n, 1, k] = grid[n % 2, lane, 1, own, :].astype(BF16)

    def pack_y(n):
        for k, lane in enumerate(Y_UP):
            y_send[n, 0, k] = grid[n % 2, lane, pl.ds(1, NX), TOP - 1, :].astype(BF16)
        for k, lane in enumerate(Y_DOWN):
            y_send[n, 1, k] = grid[n % 2, lane, pl.ds(1, NX), LOW + 1, :].astype(BF16)

    def take_all(n):
        wait_recv_all(x_copies(n))
        own = pl.ds(8, NY)
        for k, lane in enumerate(X_UP):
            grid[n % 2, lane, 0, own, :] = x_recv[n, 0, k].astype(F32)
        for k, lane in enumerate(X_DOWN):
            grid[n % 2, lane, NX + 1, own, :] = x_recv[n, 1, k].astype(F32)
        wait_recv_all(y_copies(n))
        for k, lane in enumerate(Y_UP):
            grid[n % 2, lane, pl.ds(1, NX), LOW, :] = y_recv[n, 0, k].astype(F32)
        for k, lane in enumerate(Y_DOWN):
            grid[n % 2, lane, pl.ds(1, NX), TOP, :] = y_recv[n, 1, k].astype(F32)
        wait_recv_all(c_copies(n))
        for k, (lane, cx, cy) in enumerate(CORNERS):
            x = 0 if cx > 0 else NX + 1
            y = LOW if cy > 0 else TOP
            row = 7 if cy > 0 else 0
            grid[n % 2, lane, x, pl.ds(y, 1), :] = c_recv[n, k, pl.ds(row, 1), :]

    def collide_pass(n, on_borders=None):
        @pl.loop(0, 2)
        def _(j):
            x = j * (NX - 1)
            if n == 0:
                plane_copy(x).wait()
            for yt in range(4):
                collide_block(n, x, yt)

        if on_borders is not None:
            on_borders()
        pack_x(n)
        start_all(x_copies(n))
        start_all(c_copies(n))

        @pl.loop(1, NX - 1)
        def _(x):
            if n == 0:
                plane_copy(x).wait()
            for yt in (0, 3):
                collide_block(n, x, yt)

        pack_y(n)
        start_all(y_copies(n))

        @pl.loop(1, NX - 1)
        def _(x):
            for yt in (1, 2):
                collide_block(n, x, yt)

    half_cols = 128
    my_half = pl.ds(pl.multiple_of(core * half_cols, half_cols), half_cols)

    def state_copy(d):
        to = lax.rem(slab + d, slabs)
        cols = pl.ds(pl.multiple_of(to * 256 + core * half_cols, half_cols), half_cols)
        return remote(
            state_ref.at[:, cols],
            kept.at[slab, :, my_half],
            hs_sem.at[d],
            hr_sem.at[d],
            (to, tile),
        )

    def partner_copy():
        return remote(
            kept.at[:, :, my_half],
            kept.at[:, :, my_half],
            hs_sem.at[0],
            hr_sem.at[0],
            (slab, partner),
        )

    def start_states():
        for d in range(1, slabs):
            state_copy(d).start()
        mine = pl.ds(pl.multiple_of(slab * 256 + core * half_cols, half_cols), half_cols)
        kept[slab, :, my_half] = state_ref[:, mine]

    def share_states():
        for d in range(1, slabs):
            state_copy(d).wait()
        partner_copy().start()

    def major_copy(d):
        to = lax.rem(s_major + d, majors)
        return remote(
            part.at[pl.ds(2 * to, 2)],
            part_x.at[d - 1],
            pxs_sem.at[d - 1],
            pxr_sem.at[d - 1],
            (2 * to + s_minor, tile),
        )

    def minor_copy():
        return remote(
            pair.at[1 - s_minor],
            part_y,
            pys_sem.at[0],
            pyr_sem.at[0],
            (2 * s_major + 1 - s_minor, tile),
        )

    def multiply():
        partner_copy().wait()

        @pl.loop(0, slabs)
        def _(b):
            labels = label_ref[pl.ds(b, 1), :]
            column = jnp.transpose(jnp.broadcast_to(labels, (RACKS, 128)))
            block = kept[b]
            total = jnp.zeros((RACKS, 128), F32)
            for k2 in range(KINDS // 2):
                weights = matrix_ref[pl.ds(2 * k2, 2)].reshape(256, 256)
                product = lax.dot_general(
                    block, weights, (((1,), (1,)), ((), ())), preferred_element_type=F32
                )
                total = jnp.where(column == 2 * k2, product[:, :128], total)
                total = jnp.where(column == 2 * k2 + 1, product[:, 128:], total)
            part[b] = total

        for d in range(1, majors):
            major_copy(d).start()

    def reduce_major():
        for d in range(1, majors):
            major_copy(d).wait()
        pair[...] = ((part[pl.ds(2 * s_major, 2)] + part_x[0]) + part_x[1]) + part_x[2]
        minor_copy().start()

    def finish_states():
        labels = label_ref[pl.ds(slab, 1), :]
        column = jnp.transpose(jnp.broadcast_to(labels, (RACKS, 128)))
        label_col[...] = column
        minor_copy().wait()
        cols = pl.ds(pl.multiple_of(tile * 128, 128), 128)
        base = keep_share * state_ref[:, cols].astype(F32) + (pair[s_minor] + part_y[...])
        base_ref[...] = base
        read = jnp.zeros((RACKS, 128), F32)
        for k in range(KINDS):
            read = jnp.where(column == k, read_ref[k : k + 1, cols], read)
        return jnp.sum(jnp.transpose(read * base), axis=0, keepdims=True)

    def small_copy(d):
        return remote(
            small_send,
            small_recv.at[d],
            ms_sem.at[d],
            mr_sem.at[d],
            (slab, lax.rem(tile + d, tiles)),
        )

    def after_first_borders():
        pl.semaphore_wait(barrier, (tiles - 1) + (slabs - 1) + 4)
        send_heat_rows(0)
        start_all(t_copies(0))

    solid_copy.wait()

    @pl.loop(0, NX)
    def _(x):
        heat_copy(x).wait()

    collide_pass(0, after_first_borders)
    start_states()
    heat_pass(0)
    take_all(0)
    wait_send_all(x_copies(0) + y_copies(0) + c_copies(0))

    collide_pass(1)
    share_states()
    heat_pass(1)
    multiply()
    take_all(1)
    wait_send_all(x_copies(1) + y_copies(1) + c_copies(1))

    collide_pass(2)
    heat_pass(2)

    inlet_copy.wait()
    outlet_copy.wait()
    plan, tall = face_masks(inlet_ref[...], slab, tile, tiles)
    final = warm[3, pl.ds(1, NX), pl.ds(8, NY), :].reshape(NX * NY, NZ)
    sums = jnp.dot(final, tall, precision=lax.Precision.HIGHEST, preferred_element_type=F32)
    inlet_part = jnp.sum(plan * sums, axis=0, keepdims=True)
    reduce_major()
    read_part = finish_states()
    small_send[pl.ds(0, 1), :] = inlet_part
    small_send[pl.ds(1, 1), :] = read_part
    small_send[pl.ds(2, 6), :] = jnp.zeros((6, 128), F32)

    for d in range(1, tiles):
        small_copy(d).start()

    take_all(2)

    @pl.loop(0, NX)
    def _(x):
        for i, (cx, cy, cz) in enumerate(VELOCITY):
            v = grid[0, i, x + 1 - cx, pl.ds(8 - cy, NY), :]
            f_out[i, x] = shifted_z(v, cz)

    wait_send_all(x_copies(2) + y_copies(2) + c_copies(2))

    column = label_col[...]
    cols = pl.ds(pl.multiple_of(tile * 128, 128), 128)
    gain = jnp.zeros((RACKS, 128), F32)
    for k in range(KINDS):
        gain = jnp.where(column == k, gain_ref[k : k + 1, cols], gain)
    response = jnp.sum(gain_ref[...] * read_ref[...], axis=1, keepdims=True)
    kinds = lax.broadcasted_iota(jnp.int32, (KINDS, 128), 0)
    labels = label_ref[pl.ds(slab, 1), :]
    response_row = jnp.sum(jnp.where(kinds == labels, response, 0.0), axis=0, keepdims=True)
    plan, tall = face_masks(outlet_ref[...], slab, tile, tiles)

    for d in range(1, tiles):
        small_copy(d).wait()
    total = small_send[...]
    for d in range(1, tiles):
        total = total + small_recv[d]
    inlet = total[0:1, :] * (1.0 / FACE)
    exhaust = total[1:2, :] + response_row * inlet
    states_out[...] = base_ref[...] + gain * jnp.transpose(jnp.broadcast_to(inlet, (128, RACKS)))
    dims = (((1,), (1,)), ((), ()))
    spread = lax.dot_general(
        plan * exhaust, tall, dims, precision=lax.Precision.HIGHEST, preferred_element_type=F32
    )
    inside = lax.dot_general(
        plan.astype(BF16), tall.astype(BF16), dims, preferred_element_type=F32
    )
    final = warm[3, pl.ds(1, NX), pl.ds(8, NY), :].reshape(NX * NY, NZ)
    result = final + mixing * (spread - inside * final)
    heat_out[...] = result.reshape(NX, NY, NZ)


def per_device(slabs, tiles, f, heat, solid, label, inlet, outlet, matrix, gain, read, state):
    vmem = pl.BlockSpec(memory_space=pltpu.VMEM)
    hbm = pl.BlockSpec(memory_space=pl.ANY)
    dma = pltpu.SemaphoreType.DMA
    return pl.pallas_call(
        functools.partial(kernel, slabs, tiles),
        out_shape=(
            jax.ShapeDtypeStruct((19, NX, NY, NZ), F32),
            jax.ShapeDtypeStruct((NX, NY, NZ), F32),
            jax.ShapeDtypeStruct((RACKS, 128), F32),
        ),
        in_specs=[hbm, hbm, hbm, vmem, hbm, hbm, vmem, vmem, vmem, vmem],
        out_specs=(vmem, vmem, vmem),
        scratch_shapes=[
            pltpu.VMEM((19, NX, NY, NZ), F32),
            pltpu.VMEM((2, 19, NX + 2, ROWS, NZ), F32),
            pltpu.VMEM((4, NX + 2, ROWS, NZ), F32),
            pltpu.VMEM((3, NX, NY, NZ), F32),
            pltpu.VMEM((NX, NY, NZ), jnp.int32),
            pltpu.VMEM((RACKS, FACE), jnp.int32),
            pltpu.VMEM((RACKS, FACE), jnp.int32),
            pltpu.VMEM((3, 2, 5, NY, NZ), BF16),
            pltpu.VMEM((3, 2, 5, NY, NZ), BF16),
            pltpu.VMEM((3, 2, 5, NX, NZ), BF16),
            pltpu.VMEM((3, 2, 5, NX, NZ), BF16),
            pltpu.VMEM((3, 4, 8, NZ), F32),
            pltpu.VMEM((3, 2, NX, NZ), F32),
            pltpu.VMEM((3, 2, NX, NZ), F32),
            pltpu.VMEM((slabs, RACKS, 256), BF16),
            pltpu.VMEM((RACKS, 128), jnp.int32),
            pltpu.VMEM((slabs, RACKS, 128), F32),
            pltpu.VMEM((slabs // 2 - 1, 2, RACKS, 128), F32),
            pltpu.VMEM((2, RACKS, 128), F32),
            pltpu.VMEM((RACKS, 128), F32),
            pltpu.VMEM((RACKS, 128), F32),
            pltpu.VMEM((8, 128), F32),
            pltpu.VMEM((tiles, 8, 128), F32),
            dma((NX,)),
            dma((NX,)),
            dma((3,)),
            dma((3, 2)),
            dma((3, 2)),
            dma((3, 2)),
            dma((3, 2)),
            dma((3, 4)),
            dma((3, 4)),
            dma((3, 4)),
            dma((3, 4)),
            dma((slabs,)),
            dma((slabs,)),
            dma((3,)),
            dma((3,)),
            dma((1,)),
            dma((1,)),
            dma((tiles,)),
            dma((tiles,)),
        ],
        compiler_params=pltpu.CompilerParams(
            collective_id=0, has_side_effects=True, vmem_limit_bytes=56 * 1024 * 1024
        ),
    )(f, heat, solid, label.reshape(8, 128), inlet, outlet, matrix, gain, read, state)


def solution(mesh):
    slabs, tiles = mesh.shape["slab"], mesh.shape["tile"]
    return jax.shard_map(
        functools.partial(per_device, slabs, tiles),
        mesh=mesh,
        in_specs=(
            P(None, "slab", "tile", None),
            P("slab", "tile", None),
            P("slab", "tile", None),
            P(),
            P(),
            P(),
            P(None, "tile", "slab"),
            P(),
            P(),
            P("slab", None),
        ),
        out_specs=(P(None, "slab", "tile", None), P("slab", "tile", None), P("slab", "tile")),
        check_vma=False,
    )
```

```python
import functools

import jax
import jax.numpy as jnp
from jax import lax
from jax.experimental import pallas as pl
from jax.experimental.pallas import tpu as pltpu
from jax.sharding import PartitionSpec as P

MESH = pl.DeviceIdType.MESH
F32 = jnp.float32
BF16 = jnp.bfloat16

VELOCITY = (
    (0, 0, 0),
    (1, 0, 0),
    (-1, 0, 0),
    (0, 1, 0),
    (0, -1, 0),
    (0, 0, 1),
    (0, 0, -1),
    (1, 1, 0),
    (-1, -1, 0),
    (1, -1, 0),
    (-1, 1, 0),
    (1, 0, 1),
    (-1, 0, -1),
    (1, 0, -1),
    (-1, 0, 1),
    (0, 1, 1),
    (0, -1, -1),
    (0, 1, -1),
    (0, -1, 1),
)
X_UP = (1, 7, 9, 11, 13)
X_DOWN = (2, 8, 10, 12, 14)
Y_UP = (3, 7, 10, 15, 17)
Y_DOWN = (4, 8, 9, 16, 18)
CORNERS = ((7, 1, 1), (8, -1, -1), (9, 1, -1), (10, -1, 1))

relax_time = 0.6
buoyancy = 0.01
diffusion = 0.1
mixing = 0.5
keep_share = 0.5

NX, NY, NZ = 16, 32, 128
ROWS = 48
LOW, TOP = 7, 40
KINDS = 8
RACKS = 128
FACE = 32


def collide(f, heat, solid):
    omega = 1.0 / relax_time
    keep = 1.0 - omega
    even, odd = {}, {}
    for p in range(1, 19, 2):
        even[p] = f[p] + f[p + 1]
        odd[p] = f[p] - f[p + 1]
    density = (
        f[0]
        + ((even[1] + even[3]) + (even[5] + even[7]))
        + ((even[9] + even[11]) + (even[13] + even[15]))
        + even[17]
    )
    flow_x = (odd[1] + odd[7]) + (odd[9] + odd[11]) + odd[13]
    flow_y = (odd[3] + odd[7]) + (odd[15] - odd[9]) + odd[17]
    flow_z = (odd[5] + odd[11]) + (odd[15] - odd[13]) - odd[17]
    inverse = jnp.where(solid, 0.0, 1.0 / density)
    share = jnp.where(solid, 0.0, density * (omega / 18.0))
    even_part = jnp.where(solid, 0.5, 0.5 * keep)
    odd_part = jnp.where(solid, -0.5, 0.5 * keep)
    ux = flow_x * inverse
    uy = flow_y * inverse
    uz = flow_z * inverse
    vz = (flow_z + (relax_time * buoyancy) * heat) * inverse
    bend = share * 4.5
    lean = share * 3.0
    ex, ey, ez = bend * ux, bend * uy, bend * vz
    xx, yy, zz = ex * ux, ey * uy, ez * vz
    level = share - (xx + yy + zz) * (1.0 / 3.0)
    sx, sy, sz = level + xx, level + yy, level + zz
    tx, ty, tz = lean * ux, lean * uy, lean * vz
    hx, hy, hz = 0.5 * tx, 0.5 * ty, 0.5 * tz
    mxy, mxz, myz = 0.5 * (sx + yy), 0.5 * (sx + zz), 0.5 * (sy + zz)
    qxy, qxz, qyz = ex * uy, ex * vz, ey * vz
    terms = {
        1: (sx, tx),
        3: (sy, ty),
        5: (sz, tz),
        7: (mxy + qxy, hx + hy),
        9: (mxy - qxy, hx - hy),
        11: (mxz + qxz, hx + hz),
        13: (mxz - qxz, hx - hz),
        15: (myz + qyz, hy + hz),
        17: (myz - qyz, hy - hz),
    }
    g = [None] * 19
    g[0] = f[0] * jnp.where(solid, 1.0, keep) + level * 6.0
    for p in range(1, 19, 2):
        same, turn = terms[p]
        both = even[p] * even_part + same
        half = odd[p] * odd_part + turn
        g[p] = both + half
        g[p + 1] = both - half
    return g, (ux, uy, uz)


def shifted_z(v, step):
    return pltpu.roll(v, step % NZ, 1) if step else v


def face_masks(pos, slab, tile, tiles):
    height_bits = NZ.bit_length() - 1
    across = NY * tiles
    across_bits = across.bit_length() - 1
    px = jnp.right_shift(pos, height_bits + across_bits)
    py = jnp.bitwise_and(jnp.right_shift(pos, height_bits), across - 1)
    pz = jnp.bitwise_and(pos, NZ - 1)
    least = functools.partial(jnp.min, axis=0, keepdims=True)
    x0, y0, z0 = least(px), least(py), least(pz)
    y1 = jnp.max(py, axis=0, keepdims=True)
    lifted = least(py + jnp.where(py < across // 2, across, 0))
    y0 = jnp.where(y1 - y0 > 3, lifted, y0)
    row = lax.broadcasted_iota(jnp.int32, (NX * NY, RACKS), 0)
    gx = slab * NX + jnp.right_shift(row, 5)
    gy = tile * NY + jnp.bitwise_and(row, NY - 1)
    off_y = jnp.bitwise_and(gy - y0, across - 1)
    plan = jnp.where((gx == x0) & (off_y < 4), 1.0, 0.0).astype(BF16)
    z = lax.broadcasted_iota(jnp.int32, (NZ, RACKS), 0)
    tall = jnp.where((z >= z0) & (z < z0 + 8), 1.0, 0.0).astype(BF16)
    return plan, tall


def three_parts(v):
    a = v.astype(BF16)
    rest = v - a.astype(F32)
    b = rest.astype(BF16)
    return a, b, (rest - b.astype(F32)).astype(BF16)


def kernel(
    slabs,
    tiles,
    f_hbm,
    heat_hbm,
    solid_hbm,
    label_hbm,
    inlet_hbm,
    outlet_hbm,
    matrix_hbm,
    gain_hbm,
    read_hbm,
    state_hbm,
    f_out,
    heat_out,
    states_out,
    fin,
    grid,
    warm,
    vel,
    solid_ref,
    inlet_ref,
    outlet_ref,
    label_ref,
    matrix_ref,
    gain_ref,
    read_ref,
    state_ref,
    x_send,
    x_recv,
    y_send,
    y_recv,
    c_recv,
    ty_send,
    ty_recv,
    kept,
    label_col,
    plan_in,
    tall_in,
    plan_out,
    tall_out,
    gain_rows,
    read_rows,
    response,
    part,
    part_x,
    pair,
    part_y,
    base_ref,
    small_send,
    small_recv,
    load_sem,
    heat_sem,
    misc_sem,
    xs_sem,
    xr_sem,
    ys_sem,
    yr_sem,
    cs_sem,
    cr_sem,
    tsend_sem,
    trecv_sem,
    hs_sem,
    hr_sem,
    pxs_sem,
    pxr_sem,
    pys_sem,
    pyr_sem,
    ms_sem,
    mr_sem,
):
    slab = lax.axis_index("slab")
    tile = lax.axis_index("tile")
    s_up, s_down = lax.rem(slab + 1, slabs), lax.rem(slab + slabs - 1, slabs)
    t_up, t_down = lax.rem(tile + 1, tiles), lax.rem(tile + tiles - 1, tiles)
    core = lax.rem(tile, 2)
    partner = tile + 1 - 2 * core
    s_major = slab // 2
    s_minor = lax.rem(slab, 2)
    majors = slabs // 2

    def plane_copy(x):
        return pltpu.make_async_copy(f_hbm.at[:, x], fin.at[:, x], load_sem.at[x])

    def heat_copy(x):
        return pltpu.make_async_copy(
            heat_hbm.at[x], warm.at[0, x + 1, pl.ds(8, NY), :], heat_sem.at[x]
        )

    solid_copy = pltpu.make_async_copy(solid_hbm, solid_ref, misc_sem.at[0])
    first_rack = pl.multiple_of(slab * RACKS, RACKS)
    inlet_copy = pltpu.make_async_copy(
        inlet_hbm.at[:, pl.ds(first_rack, RACKS)], inlet_ref, misc_sem.at[1]
    )
    outlet_copy = pltpu.make_async_copy(
        outlet_hbm.at[:, pl.ds(first_rack, RACKS)], outlet_ref, misc_sem.at[2]
    )
    solid_copy.start()

    @pl.loop(0, NX)
    def _(x):
        heat_copy(x).start()

    plane_copy(0).start()
    plane_copy(NX - 1).start()

    @pl.loop(1, NX - 1)
    def _(x):
        plane_copy(x).start()

    label_copy = pltpu.make_async_copy(label_hbm, label_ref, misc_sem.at[3])
    matrix_copy = pltpu.make_async_copy(matrix_hbm, matrix_ref, misc_sem.at[4])
    gain_copy = pltpu.make_async_copy(gain_hbm, gain_ref, misc_sem.at[5])
    read_copy = pltpu.make_async_copy(read_hbm, read_ref, misc_sem.at[6])
    state_copy_in = pltpu.make_async_copy(state_hbm, state_ref, misc_sem.at[7])
    state_copy_in.start()
    table_copies = (label_copy, inlet_copy, outlet_copy, gain_copy, read_copy, matrix_copy)
    for c in table_copies:
        c.start()

    barrier = pltpu.get_barrier_semaphore()

    @pl.loop(1, tiles)
    def _(d):
        pl.semaphore_signal(
            barrier, inc=1, device_id=(slab, lax.rem(tile + d, tiles)), device_id_type=MESH
        )

    @pl.loop(1, slabs)
    def _(d):
        pl.semaphore_signal(
            barrier, inc=1, device_id=(lax.rem(slab + d, slabs), tile), device_id_type=MESH
        )

    for ds in (s_up, s_down):
        for dt in (t_up, t_down):
            pl.semaphore_signal(barrier, inc=1, device_id=(ds, dt), device_id_type=MESH)

    def remote(src, dst, send, recv, to):
        return pltpu.make_async_remote_copy(
            src_ref=src,
            dst_ref=dst,
            send_sem=send,
            recv_sem=recv,
            device_id=to,
            device_id_type=MESH,
        )

    def x_copies(n):
        return [
            remote(x_send.at[n, 0], x_recv.at[n, 0], xs_sem.at[n, 0], xr_sem.at[n, 0], (s_up, tile)),
            remote(x_send.at[n, 1], x_recv.at[n, 1], xs_sem.at[n, 1], xr_sem.at[n, 1], (s_down, tile)),
        ]

    def y_copies(n):
        return [
            remote(y_send.at[n, 0], y_recv.at[n, 0], ys_sem.at[n, 0], yr_sem.at[n, 0], (slab, t_up)),
            remote(y_send.at[n, 1], y_recv.at[n, 1], ys_sem.at[n, 1], yr_sem.at[n, 1], (slab, t_down)),
        ]

    def c_copies(n):
        out = []
        for k, (lane, cx, cy) in enumerate(CORNERS):
            x = NX if cx > 0 else 1
            y = TOP - 8 if cy > 0 else LOW + 1
            to = (s_up if cx > 0 else s_down, t_up if cy > 0 else t_down)
            out.append(
                remote(
                    grid.at[n % 2, lane, x, pl.ds(y, 8), :],
                    c_recv.at[n, k],
                    cs_sem.at[n, k],
                    cr_sem.at[n, k],
                    to,
                )
            )
        return out

    def t_copies(n):
        own = pl.ds(8, NY)
        return [
            remote(
                warm.at[n, NX, own, :],
                warm.at[n, 0, own, :],
                tsend_sem.at[n, 0],
                trecv_sem.at[n, 0],
                (s_up, tile),
            ),
            remote(
                warm.at[n, 1, own, :],
                warm.at[n, NX + 1, own, :],
                tsend_sem.at[n, 1],
                trecv_sem.at[n, 1],
                (s_down, tile),
            ),
            remote(ty_send.at[n, 0], ty_recv.at[n, 0], tsend_sem.at[n, 2], trecv_sem.at[n, 2], (slab, t_up)),
            remote(ty_send.at[n, 1], ty_recv.at[n, 1], tsend_sem.at[n, 3], trecv_sem.at[n, 3], (slab, t_down)),
        ]

    def start_all(copies):
        for c in copies:
            c.start()

    def wait_recv_all(copies):
        for c in copies:
            c.wait_recv()

    def wait_send_all(copies):
        for c in copies:
            c.wait_send()

    def collide_block(n, x, yt):
        rows = pl.ds(8 + 8 * yt, 8)
        here = pl.ds(8 * yt, 8)
        if n == 0:
            f = [fin[i, x, here, :] for i in range(19)]
        else:
            old = (n - 1) % 2
            f = []
            for i, (cx, cy, cz) in enumerate(VELOCITY):
                v = grid[old, i, x + 1 - cx, pl.ds(8 + 8 * yt - cy, 8), :]
                f.append(shifted_z(v, cz))
        heat = warm[n, x + 1, rows, :]
        solid = solid_ref[x, here, :] == 1
        g, u = collide(f, heat, solid)
        new = n % 2
        for i in range(19):
            grid[new, i, x + 1, rows, :] = g[i]
        for d in range(3):
            vel[d, x, here, :] = u[d]

    def heat_block(n, x, yt):
        rows = pl.ds(8 + 8 * yt, 8)
        here = pl.ds(8 * yt, 8)
        centre = warm[n, x + 1, rows, :]
        pairs = (
            (warm[n, x, rows, :], warm[n, x + 2, rows, :]),
            (
                warm[n, x + 1, pl.ds(7 + 8 * yt, 8), :],
                warm[n, x + 1, pl.ds(9 + 8 * yt, 8), :],
            ),
            (shifted_z(centre, 1), shifted_z(centre, -1)),
        )
        laplace = -6.0 * centre
        carried = None
        for d in range(3):
            behind, ahead = pairs[d]
            laplace = laplace + (behind + ahead)
            term = vel[d, x, here, :] * (0.5 * (ahead - behind))
            carried = term if carried is None else carried + term
        solid = solid_ref[x, here, :] == 1
        warm[n + 1, x + 1, rows, :] = jnp.where(solid, centre, centre + diffusion * laplace - carried)

    def send_heat_rows(n):
        ty_send[n, 0] = warm[n, pl.ds(1, NX), TOP - 1, :]
        ty_send[n, 1] = warm[n, pl.ds(1, NX), LOW + 1, :]

    def take_heat_rows(n):
        warm[n, pl.ds(1, NX), LOW, :] = ty_recv[n, 0]
        warm[n, pl.ds(1, NX), TOP, :] = ty_recv[n, 1]

    def heat_pass(n):
        copies = t_copies(n)
        wait_recv_all(copies)
        take_heat_rows(n)

        @pl.loop(0, NX)
        def _(x):
            for yt in range(4):
                heat_block(n, x, yt)

        wait_send_all(copies)
        if n < 2:
            send_heat_rows(n + 1)
            start_all(t_copies(n + 1))

    def pack_x(n):
        own = pl.ds(8, NY)
        for k, lane in enumerate(X_UP):
            x_send[n, 0, k] = grid[n % 2, lane, NX, own, :].astype(BF16)
        for k, lane in enumerate(X_DOWN):
            x_send[n, 1, k] = grid[n % 2, lane, 1, own, :].astype(BF16)

    def pack_y(n):
        for k, lane in enumerate(Y_UP):
            y_send[n, 0, k] = grid[n % 2, lane, pl.ds(1, NX), TOP - 1, :].astype(BF16)
        for k, lane in enumerate(Y_DOWN):
            y_send[n, 1, k] = grid[n % 2, lane, pl.ds(1, NX), LOW + 1, :].astype(BF16)

    def take_all(n):
        wait_recv_all(x_copies(n))
        own = pl.ds(8, NY)
        for k, lane in enumerate(X_UP):
            grid[n % 2, lane, 0, own, :] = x_recv[n, 0, k].astype(F32)
        for k, lane in enumerate(X_DOWN):
            grid[n % 2, lane, NX + 1, own, :] = x_recv[n, 1, k].astype(F32)
        wait_recv_all(y_copies(n))
        for k, lane in enumerate(Y_UP):
            grid[n % 2, lane, pl.ds(1, NX), LOW, :] = y_recv[n, 0, k].astype(F32)
        for k, lane in enumerate(Y_DOWN):
            grid[n % 2, lane, pl.ds(1, NX), TOP, :] = y_recv[n, 1, k].astype(F32)
        wait_recv_all(c_copies(n))
        for k, (lane, cx, cy) in enumerate(CORNERS):
            x = 0 if cx > 0 else NX + 1
            y = LOW if cy > 0 else TOP
            row = 7 if cy > 0 else 0
            grid[n % 2, lane, x, pl.ds(y, 1), :] = c_recv[n, k, pl.ds(row, 1), :]

    def edges(n):
        @pl.loop(0, 2)
        def _(j):
            x = j * (NX - 1)
            if n == 0:
                plane_copy(x).wait()
            for yt in range(4):
                collide_block(n, x, yt)

    def rims(n):
        @pl.loop(1, NX - 1)
        def _(x):
            if n == 0:
                plane_copy(x).wait()
            for yt in (0, 3):
                collide_block(n, x, yt)

    def middle(n):
        @pl.loop(1, NX - 1)
        def _(x):
            for yt in (1, 2):
                collide_block(n, x, yt)

    def send_x(n):
        pack_x(n)
        start_all(x_copies(n))
        start_all(c_copies(n))

    def send_y(n):
        pack_y(n)
        start_all(y_copies(n))

    half_cols = 128
    my_half = pl.ds(pl.multiple_of(core * half_cols, half_cols), half_cols)

    def state_copy(d):
        to = lax.rem(slab + d, slabs)
        cols = pl.ds(pl.multiple_of(to * 256 + core * half_cols, half_cols), half_cols)
        return remote(
            state_ref.at[:, cols],
            kept.at[slab, :, my_half],
            hs_sem.at[d],
            hr_sem.at[d],
            (to, tile),
        )

    def partner_copy():
        return remote(
            kept.at[:, :, my_half],
            kept.at[:, :, my_half],
            hs_sem.at[0],
            hr_sem.at[0],
            (slab, partner),
        )

    def start_states():
        for d in range(1, slabs):
            state_copy(d).start()
        mine = pl.ds(pl.multiple_of(slab * 256 + core * half_cols, half_cols), half_cols)
        kept[slab, :, my_half] = state_ref[:, mine]

    def share_states():
        for d in range(1, slabs):
            state_copy(d).wait()
        partner_copy().start()

    def major_copy(d):
        to = lax.rem(s_major + d, majors)
        return remote(
            part.at[pl.ds(2 * to, 2)],
            part_x.at[d - 1],
            pxs_sem.at[d - 1],
            pxr_sem.at[d - 1],
            (2 * to + s_minor, tile),
        )

    def minor_copy():
        return remote(
            pair.at[1 - s_minor],
            part_y,
            pys_sem.at[0],
            pyr_sem.at[0],
            (2 * s_major + 1 - s_minor, tile),
        )

    def multiply():
        partner_copy().wait()

        rows = 256

        @pl.loop(0, slabs * RACKS // rows)
        def _(m):
            block = kept[pl.ds(2 * m, 2)].reshape(rows, 256)
            column = label_col[pl.ds(pl.multiple_of(m * rows, rows), rows), :]
            total = jnp.zeros((rows, 128), F32)
            for k2 in range(KINDS // 2):
                weights = matrix_ref[pl.ds(2 * k2, 2)].reshape(256, 256)
                product = lax.dot_general(
                    block, weights, (((1,), (1,)), ((), ())), preferred_element_type=F32
                )
                total = jnp.where(column == 2 * k2, product[:, :128], total)
                total = jnp.where(column == 2 * k2 + 1, product[:, 128:], total)
            part[pl.ds(2 * m, 2)] = total.reshape(2, RACKS, 128)

        for d in range(1, majors):
            major_copy(d).start()

    def reduce_major():
        for d in range(1, majors):
            major_copy(d).wait()
        pair[...] = ((part[pl.ds(2 * s_major, 2)] + part_x[0]) + part_x[1]) + part_x[2]
        minor_copy().start()

    def tables():
        for c in table_copies:
            c.wait()
        plan_in[...], tall_in[...] = face_masks(inlet_ref[...], slab, tile, tiles)
        plan_out[...], tall_out[...] = face_masks(outlet_ref[...], slab, tile, tiles)

        @pl.loop(0, slabs)
        def _(b):
            labels = label_ref[pl.ds(b, 1), :]
            rows = pl.ds(pl.multiple_of(b * RACKS, RACKS), RACKS)
            label_col[rows, :] = jnp.transpose(jnp.broadcast_to(labels, (RACKS, 128)))

        column = label_col[pl.ds(first_rack, RACKS), :]
        cols = pl.ds(pl.multiple_of(tile * 128, 128), 128)
        gain = jnp.zeros((RACKS, 128), F32)
        read = jnp.zeros((RACKS, 128), F32)
        for k in range(KINDS):
            gain = jnp.where(column == k, gain_ref[k : k + 1, cols], gain)
            read = jnp.where(column == k, read_ref[k : k + 1, cols], read)
        gain_rows[...] = gain
        read_rows[...] = read
        per_kind = jnp.sum(gain_ref[...] * read_ref[...], axis=1, keepdims=True)
        kinds = lax.broadcasted_iota(jnp.int32, (KINDS, 128), 0)
        labels = label_ref[pl.ds(slab, 1), :]
        row = jnp.sum(jnp.where(kinds == labels, per_kind, 0.0), axis=0, keepdims=True)
        response[...] = jnp.broadcast_to(row, (8, 128))

    def finish_states():
        minor_copy().wait()
        cols = pl.ds(pl.multiple_of(tile * 128, 128), 128)
        base = keep_share * state_ref[:, cols].astype(F32) + (pair[s_minor] + part_y[...])
        base_ref[...] = base
        return jnp.sum(jnp.transpose(read_rows[...] * base), axis=0, keepdims=True)

    def small_copy(d):
        return remote(
            small_send,
            small_recv.at[d],
            ms_sem.at[d],
            mr_sem.at[d],
            (slab, lax.rem(tile + d, tiles)),
        )

    def stream_plane(x):
        for i, (cx, cy, cz) in enumerate(VELOCITY):
            v = grid[0, i, x + 1 - cx, pl.ds(8 - cy, NY), :]
            f_out[i, x] = shifted_z(v, cz)

    solid_copy.wait()

    @pl.loop(0, NX)
    def _(x):
        heat_copy(x).wait()

    edges(0)
    rims(0)
    pl.semaphore_wait(barrier, (tiles - 1) + (slabs - 1) + 4)
    send_heat_rows(0)
    start_all(t_copies(0))
    send_x(0)
    send_y(0)
    state_copy_in.wait()
    start_states()
    middle(0)
    tables()
    heat_pass(0)
    share_states()
    take_all(0)
    wait_send_all(x_copies(0) + y_copies(0) + c_copies(0))

    edges(1)
    send_x(1)
    rims(1)
    send_y(1)
    multiply()
    middle(1)
    heat_pass(1)
    take_all(1)
    wait_send_all(x_copies(1) + y_copies(1) + c_copies(1))

    edges(2)
    send_x(2)
    rims(2)
    send_y(2)
    reduce_major()
    middle(2)
    heat_pass(2)

    final = warm[3, pl.ds(1, NX), pl.ds(8, NY), :].reshape(NX * NY, NZ)
    sums = jnp.zeros((NX * NY, RACKS), F32)
    for piece in three_parts(final):
        sums = sums + jnp.dot(piece, tall_in[...], preferred_element_type=F32)
    inlet_part = jnp.sum(plan_in[...].astype(F32) * sums, axis=0, keepdims=True)
    read_part = finish_states()
    small_send[pl.ds(0, 1), :] = inlet_part
    small_send[pl.ds(1, 1), :] = read_part
    small_send[pl.ds(2, 6), :] = jnp.zeros((6, 128), F32)

    for d in range(1, tiles):
        small_copy(d).start()

    dims = (((1,), (1,)), ((), ()))
    inside = lax.dot_general(plan_out[...], tall_out[...], dims, preferred_element_type=F32)
    final = warm[3, pl.ds(1, NX), pl.ds(8, NY), :].reshape(NX * NY, NZ)
    heat_out[...] = (final - mixing * (inside * final)).reshape(NX, NY, NZ)

    @pl.loop(1, NX - 1)
    def _(x):
        stream_plane(x)

    take_all(2)

    @pl.loop(0, 2)
    def _(j):
        stream_plane(j * (NX - 1))

    for lanes, halo, row in ((Y_UP, LOW, 0), (Y_DOWN, TOP, NY - 1)):
        for lane in lanes:
            cx, _, cz = VELOCITY[lane]
            v = grid[0, lane, pl.ds(1 - cx, NX), halo, :]
            f_out[lane, :, row, :] = shifted_z(v, cz)

    wait_send_all(x_copies(2) + y_copies(2) + c_copies(2))

    for d in range(1, tiles):
        small_copy(d).wait()
    total = small_send[...]
    for d in range(1, tiles):
        total = total + small_recv[d]
    inlet = total[0:1, :] * (1.0 / FACE)
    exhaust = mixing * (total[1:2, :] + response[0:1, :] * inlet)
    spread = jnp.zeros((NX * NY, NZ), F32)
    for piece in three_parts(exhaust):
        spread = spread + lax.dot_general(
            plan_out[...], tall_out[...] * piece, dims, preferred_element_type=F32
        )
    heat_out[...] = heat_out[...] + spread.reshape(NX, NY, NZ)
    inlets = jnp.transpose(jnp.broadcast_to(inlet, (128, RACKS)))
    states_out[...] = base_ref[...] + gain_rows[...] * inlets


def flush(f_ref, heat_ref, states_ref, f_out, heat_out, states_out, sems):
    copies = [
        pltpu.make_async_copy(heat_ref, heat_out, sems.at[19]),
        pltpu.make_async_copy(states_ref, states_out, sems.at[20]),
    ]
    for i in range(19):
        copies.append(pltpu.make_async_copy(f_ref.at[i], f_out.at[i], sems.at[i]))
    for c in copies:
        c.start()
    for c in copies:
        c.wait()


def per_device(slabs, tiles, f, heat, solid, label, inlet, outlet, matrix, gain, read, state):
    vmem = pl.BlockSpec(memory_space=pltpu.VMEM)
    hbm = pl.BlockSpec(memory_space=pltpu.HBM)
    dma = pltpu.SemaphoreType.DMA
    results = ((19, NX, NY, NZ), (NX, NY, NZ), (RACKS, 128))
    operands = (f, heat, solid, label.reshape(8, 128), inlet.T, outlet.T, matrix, gain, read, state)
    outs = pl.pallas_call(
        functools.partial(kernel, slabs, tiles),
        out_shape=tuple(pltpu.VMEM(shape, F32) for shape in results),
        in_specs=[hbm] * 10,
        out_specs=(vmem, vmem, vmem),
        scratch_shapes=[
            pltpu.VMEM((19, NX, NY, NZ), F32),
            pltpu.VMEM((2, 19, NX + 2, ROWS, NZ), F32),
            pltpu.VMEM((4, NX + 2, ROWS, NZ), F32),
            pltpu.VMEM((3, NX, NY, NZ), F32),
            pltpu.VMEM((NX, NY, NZ), jnp.int32),
            pltpu.VMEM((FACE, RACKS), jnp.int32),
            pltpu.VMEM((FACE, RACKS), jnp.int32),
            pltpu.VMEM((slabs, 128), jnp.int32),
            pltpu.VMEM((KINDS, 128, 256), BF16),
            pltpu.VMEM((KINDS, tiles * 128), F32),
            pltpu.VMEM((KINDS, tiles * 128), F32),
            pltpu.VMEM((RACKS, tiles * 128), BF16),
            pltpu.VMEM((3, 2, 5, NY, NZ), BF16),
            pltpu.VMEM((3, 2, 5, NY, NZ), BF16),
            pltpu.VMEM((3, 2, 5, NX, NZ), BF16),
            pltpu.VMEM((3, 2, 5, NX, NZ), BF16),
            pltpu.VMEM((3, 4, 8, NZ), F32),
            pltpu.VMEM((3, 2, NX, NZ), F32),
            pltpu.VMEM((3, 2, NX, NZ), F32),
            pltpu.VMEM((slabs, RACKS, 256), BF16),
            pltpu.VMEM((slabs * RACKS, 128), jnp.int32),
            pltpu.VMEM((NX * NY, RACKS), BF16),
            pltpu.VMEM((NZ, RACKS), BF16),
            pltpu.VMEM((NX * NY, RACKS), BF16),
            pltpu.VMEM((NZ, RACKS), BF16),
            pltpu.VMEM((RACKS, 128), F32),
            pltpu.VMEM((RACKS, 128), F32),
            pltpu.VMEM((8, 128), F32),
            pltpu.VMEM((slabs, RACKS, 128), F32),
            pltpu.VMEM((slabs // 2 - 1, 2, RACKS, 128), F32),
            pltpu.VMEM((2, RACKS, 128), F32),
            pltpu.VMEM((RACKS, 128), F32),
            pltpu.VMEM((RACKS, 128), F32),
            pltpu.VMEM((8, 128), F32),
            pltpu.VMEM((tiles, 8, 128), F32),
            dma((NX,)),
            dma((NX,)),
            dma((8,)),
            dma((3, 2)),
            dma((3, 2)),
            dma((3, 2)),
            dma((3, 2)),
            dma((3, 4)),
            dma((3, 4)),
            dma((3, 4)),
            dma((3, 4)),
            dma((slabs,)),
            dma((slabs,)),
            dma((3,)),
            dma((3,)),
            dma((1,)),
            dma((1,)),
            dma((tiles,)),
            dma((tiles,)),
        ],
        compiler_params=pltpu.CompilerParams(
            collective_id=0, has_side_effects=True, vmem_limit_bytes=40 * 1024 * 1024
        ),
    )(*(pltpu.with_memory_space_constraint(a, pltpu.HBM) for a in operands))
    return pl.pallas_call(
        flush,
        out_shape=tuple(jax.ShapeDtypeStruct(shape, F32) for shape in results),
        in_specs=[vmem] * 3,
        out_specs=(hbm,) * 3,
        scratch_shapes=[dma((21,))],
        compiler_params=pltpu.CompilerParams(vmem_limit_bytes=1024 * 1024),
    )(*outs)


def solution(mesh):
    slabs, tiles = mesh.shape["slab"], mesh.shape["tile"]
    return jax.shard_map(
        functools.partial(per_device, slabs, tiles),
        mesh=mesh,
        in_specs=(
            P(None, "slab", "tile", None),
            P("slab", "tile", None),
            P("slab", "tile", None),
            P(),
            P(),
            P(),
            P(None, "tile", "slab"),
            P(),
            P(),
            P("slab", None),
        ),
        out_specs=(P(None, "slab", "tile", None), P("slab", "tile", None), P("slab", "tile")),
        check_vma=False,
    )
```

```python
import functools

import jax
import jax.numpy as jnp
from jax import lax
from jax.experimental import pallas as pl
from jax.experimental.pallas import tpu as pltpu
from jax.sharding import PartitionSpec as P

MESH = pl.DeviceIdType.MESH
F32 = jnp.float32
BF16 = jnp.bfloat16

VELOCITY = (
    (0, 0, 0),
    (1, 0, 0),
    (-1, 0, 0),
    (0, 1, 0),
    (0, -1, 0),
    (0, 0, 1),
    (0, 0, -1),
    (1, 1, 0),
    (-1, -1, 0),
    (1, -1, 0),
    (-1, 1, 0),
    (1, 0, 1),
    (-1, 0, -1),
    (1, 0, -1),
    (-1, 0, 1),
    (0, 1, 1),
    (0, -1, -1),
    (0, 1, -1),
    (0, -1, 1),
)
X_UP = (1, 7, 9, 11, 13)
X_DOWN = (2, 8, 10, 12, 14)
Y_UP = (3, 7, 10, 15, 17)
Y_DOWN = (4, 8, 9, 16, 18)
CORNERS = ((7, 1, 1), (8, -1, -1), (9, 1, -1), (10, -1, 1))

relax_time = 0.6
buoyancy = 0.01
diffusion = 0.1
mixing = 0.5
keep_share = 0.5

NX, NY, NZ = 16, 32, 128
ROWS = 48
LOW, TOP = 7, 40
KINDS = 8
RACKS = 128
FACE = 32


def gather_moments(f):
    even = [f[p] + f[p + 1] for p in range(1, 19, 2)]
    odd = [f[p] - f[p + 1] for p in range(1, 19, 2)]
    density = (
        f[0]
        + ((even[0] + even[1]) + (even[2] + even[3]))
        + ((even[4] + even[5]) + (even[6] + even[7]))
        + even[8]
    )
    flow_x = (odd[0] + odd[3]) + (odd[4] + odd[5]) + odd[6]
    flow_y = (odd[1] + odd[3]) + (odd[7] - odd[4]) + odd[8]
    flow_z = (odd[2] + odd[5]) + (odd[7] - odd[6]) - odd[8]
    return f[0], even, odd, density, flow_x, flow_y, flow_z


def relax(still, even, odd, density, flow_x, flow_y, flow_z, heat, solid):
    omega = 1.0 / relax_time
    keep = 1.0 - omega
    inverse = jnp.where(solid, 0.0, 1.0 / density)
    share = jnp.where(solid, 0.0, density * (omega / 18.0))
    even_part = jnp.where(solid, 0.5, 0.5 * keep)
    odd_part = jnp.where(solid, -0.5, 0.5 * keep)
    ux = flow_x * inverse
    uy = flow_y * inverse
    uz = flow_z * inverse
    vz = (flow_z + (relax_time * buoyancy) * heat) * inverse
    bend = share * 4.5
    lean = share * 3.0
    ex, ey, ez = bend * ux, bend * uy, bend * vz
    xx, yy, zz = ex * ux, ey * uy, ez * vz
    level = share - (xx + yy + zz) * (1.0 / 3.0)
    sx, sy, sz = level + xx, level + yy, level + zz
    tx, ty, tz = lean * ux, lean * uy, lean * vz
    hx, hy, hz = 0.5 * tx, 0.5 * ty, 0.5 * tz
    mxy, mxz, myz = 0.5 * (sx + yy), 0.5 * (sx + zz), 0.5 * (sy + zz)
    qxy, qxz, qyz = ex * uy, ex * vz, ey * vz
    terms = {
        1: (sx, tx),
        3: (sy, ty),
        5: (sz, tz),
        7: (mxy + qxy, hx + hy),
        9: (mxy - qxy, hx - hy),
        11: (mxz + qxz, hx + hz),
        13: (mxz - qxz, hx - hz),
        15: (myz + qyz, hy + hz),
        17: (myz - qyz, hy - hz),
    }
    g = [None] * 19
    g[0] = still * jnp.where(solid, 1.0, keep) + level * 6.0
    for p in range(1, 19, 2):
        same, turn = terms[p]
        both = even[p // 2] * even_part + same
        half = odd[p // 2] * odd_part + turn
        g[p] = both + half
        g[p + 1] = both - half
    return g, (ux, uy, uz)


def shifted_z(v, step):
    return pltpu.roll(v, step % NZ, 1) if step else v


def face_masks(pos, slab, tile, tiles):
    height_bits = NZ.bit_length() - 1
    across = NY * tiles
    across_bits = across.bit_length() - 1
    px = jnp.right_shift(pos, height_bits + across_bits)
    py = jnp.bitwise_and(jnp.right_shift(pos, height_bits), across - 1)
    pz = jnp.bitwise_and(pos, NZ - 1)
    least = functools.partial(jnp.min, axis=0, keepdims=True)
    x0, y0, z0 = least(px), least(py), least(pz)
    y1 = jnp.max(py, axis=0, keepdims=True)
    lifted = least(py + jnp.where(py < across // 2, across, 0))
    y0 = jnp.where(y1 - y0 > 3, lifted, y0)
    row = lax.broadcasted_iota(jnp.int32, (NX * NY, RACKS), 0)
    gx = slab * NX + jnp.right_shift(row, 5)
    gy = tile * NY + jnp.bitwise_and(row, NY - 1)
    off_y = jnp.bitwise_and(gy - y0, across - 1)
    plan = jnp.where((gx == x0) & (off_y < 4), 1.0, 0.0).astype(BF16)
    z = lax.broadcasted_iota(jnp.int32, (NZ, RACKS), 0)
    tall = jnp.where((z >= z0) & (z < z0 + 8), 1.0, 0.0).astype(BF16)
    return plan, tall


def three_parts(v):
    a = v.astype(BF16)
    rest = v - a.astype(F32)
    b = rest.astype(BF16)
    return a, b, (rest - b.astype(F32)).astype(BF16)


def kernel(
    slabs,
    tiles,
    f_hbm,
    heat_hbm,
    solid_hbm,
    label_hbm,
    inlet_hbm,
    outlet_hbm,
    matrix_hbm,
    gain_hbm,
    read_hbm,
    state_hbm,
    f_out,
    heat_out,
    states_out,
    fin,
    grid_even,
    grid_odd,
    warm,
    vel,
    mid,
    solid_ref,
    inlet_ref,
    outlet_ref,
    label_ref,
    matrix_ref,
    gain_ref,
    read_ref,
    state_ref,
    x_send,
    x_recv,
    y_send,
    y_recv,
    c_recv,
    ty_send,
    ty_recv,
    kept,
    label_col,
    plan_in,
    tall_in,
    plan_out,
    tall_out,
    gain_rows,
    read_rows,
    response,
    part,
    part_x,
    pair,
    part_y,
    cross_send,
    cross_recv,
    small_send,
    small_recv,
    load_sem,
    heat_sem,
    misc_sem,
    xs_sem,
    xr_sem,
    ys_sem,
    yr_sem,
    cs_sem,
    cr_sem,
    tsend_sem,
    trecv_sem,
    hs_sem,
    hr_sem,
    pxs_sem,
    pxr_sem,
    pys_sem,
    pyr_sem,
    ms_sem,
    mr_sem,
):
    grids = (grid_even, grid_odd)
    flats = [g.reshape(19, (NX + 2) * ROWS, NZ) for g in grids]
    warm_flat = warm.reshape(4, (NX + 2) * ROWS, NZ)
    fin_flat = fin.reshape(19, NX * NY, NZ)
    solid_flat = solid_ref.reshape(NX * NY, NZ)

    def along_x(row, first=1, count=NX):
        return pl.ds(first * ROWS + row, count, stride=ROWS)

    slab = lax.axis_index("slab")
    tile = lax.axis_index("tile")
    s_up, s_down = lax.rem(slab + 1, slabs), lax.rem(slab + slabs - 1, slabs)
    t_up, t_down = lax.rem(tile + 1, tiles), lax.rem(tile + tiles - 1, tiles)
    core = lax.rem(tile, 2)
    partner = tile + 1 - 2 * core
    s_major = slab // 2
    s_minor = lax.rem(slab, 2)
    majors = slabs // 2

    def plane_copy(x):
        return pltpu.make_async_copy(f_hbm.at[:, x], fin.at[:, x], load_sem.at[x])

    heat_copy = pltpu.make_async_copy(
        heat_hbm, warm.at[0, pl.ds(1, NX), pl.ds(8, NY), :], heat_sem.at[0]
    )

    solid_copy = pltpu.make_async_copy(solid_hbm, solid_ref, misc_sem.at[0])
    first_rack = pl.multiple_of(slab * RACKS, RACKS)
    inlet_copy = pltpu.make_async_copy(
        inlet_hbm.at[:, pl.ds(first_rack, RACKS)], inlet_ref, misc_sem.at[1]
    )
    outlet_copy = pltpu.make_async_copy(
        outlet_hbm.at[:, pl.ds(first_rack, RACKS)], outlet_ref, misc_sem.at[2]
    )
    solid_copy.start()

    heat_copy.start()
    plane_copy(0).start()
    plane_copy(NX - 1).start()
    state_copy_in = pltpu.make_async_copy(state_hbm, state_ref, misc_sem.at[7])
    state_copy_in.start()

    @pl.loop(1, NX - 1)
    def _(x):
        plane_copy(x).start()

    label_copy = pltpu.make_async_copy(label_hbm, label_ref, misc_sem.at[3])
    matrix_copy = pltpu.make_async_copy(matrix_hbm, matrix_ref, misc_sem.at[4])
    gain_copy = pltpu.make_async_copy(gain_hbm, gain_ref, misc_sem.at[5])
    read_copy = pltpu.make_async_copy(read_hbm, read_ref, misc_sem.at[6])
    table_copies = (label_copy, inlet_copy, outlet_copy, gain_copy, read_copy, matrix_copy)
    for c in table_copies:
        c.start()

    barrier = pltpu.get_barrier_semaphore()

    @pl.loop(1, tiles)
    def _(d):
        pl.semaphore_signal(
            barrier, inc=1, device_id=(slab, lax.rem(tile + d, tiles)), device_id_type=MESH
        )

    @pl.loop(1, slabs)
    def _(d):
        pl.semaphore_signal(
            barrier, inc=1, device_id=(lax.rem(slab + d, slabs), tile), device_id_type=MESH
        )

    @pl.loop(1, tiles)
    def _(d):
        to = (slab + 1 - 2 * s_minor, lax.rem(tile + d, tiles))
        pl.semaphore_signal(barrier, inc=1, device_id=to, device_id_type=MESH)

    for ds in (s_up, s_down):
        for dt in (t_up, t_down):
            pl.semaphore_signal(barrier, inc=1, device_id=(ds, dt), device_id_type=MESH)

    def remote(src, dst, send, recv, to):
        return pltpu.make_async_remote_copy(
            src_ref=src,
            dst_ref=dst,
            send_sem=send,
            recv_sem=recv,
            device_id=to,
            device_id_type=MESH,
        )

    def x_copies(n):
        return [
            remote(x_send.at[n, 0], x_recv.at[n, 0], xs_sem.at[n, 0], xr_sem.at[n, 0], (s_up, tile)),
            remote(x_send.at[n, 1], x_recv.at[n, 1], xs_sem.at[n, 1], xr_sem.at[n, 1], (s_down, tile)),
        ]

    def y_copies(n):
        return [
            remote(y_send.at[n, 0], y_recv.at[n, 0], ys_sem.at[n, 0], yr_sem.at[n, 0], (slab, t_up)),
            remote(y_send.at[n, 1], y_recv.at[n, 1], ys_sem.at[n, 1], yr_sem.at[n, 1], (slab, t_down)),
        ]

    def c_copies(n):
        out = []
        for k, (lane, cx, cy) in enumerate(CORNERS):
            x = NX if cx > 0 else 1
            y = TOP - 8 if cy > 0 else LOW + 1
            to = (s_up if cx > 0 else s_down, t_up if cy > 0 else t_down)
            out.append(
                remote(
                    grids[n % 2].at[lane, x, pl.ds(y, 8), :],
                    c_recv.at[n, k],
                    cs_sem.at[n, k],
                    cr_sem.at[n, k],
                    to,
                )
            )
        return out

    def t_copies(n):
        own = pl.ds(8, NY)
        return [
            remote(
                warm.at[n, NX, own, :],
                warm.at[n, 0, own, :],
                tsend_sem.at[n, 0],
                trecv_sem.at[n, 0],
                (s_up, tile),
            ),
            remote(
                warm.at[n, 1, own, :],
                warm.at[n, NX + 1, own, :],
                tsend_sem.at[n, 1],
                trecv_sem.at[n, 1],
                (s_down, tile),
            ),
            remote(ty_send.at[n, 0], ty_recv.at[n, 0], tsend_sem.at[n, 2], trecv_sem.at[n, 2], (slab, t_up)),
            remote(ty_send.at[n, 1], ty_recv.at[n, 1], tsend_sem.at[n, 3], trecv_sem.at[n, 3], (slab, t_down)),
        ]

    def start_all(copies):
        for c in copies:
            c.start()

    def wait_recv_all(copies):
        for c in copies:
            c.wait_recv()

    def wait_send_all(copies):
        for c in copies:
            c.wait_send()

    def keep_moments(slot, f):
        still, even, odd, density, *flow = gather_moments(f)
        for i, v in enumerate((still, density, *flow, *even, *odd)):
            mid[slot, i] = v

    def relax_kept(slot, heat, solid):
        even = [mid[slot, 5 + i] for i in range(9)]
        odd = [mid[slot, 14 + i] for i in range(9)]
        still, density, *flow = [mid[slot, i] for i in range(5)]
        return relax(still, even, odd, density, *flow, heat, solid)

    def moments(n, blocks):
        for k, (x, yt) in enumerate(blocks):
            here = pl.ds(8 * yt, 8)
            if n == 0:
                f = [fin[i, x, here, :] for i in range(19)]
            else:
                f = []
                for i, (cx, cy, cz) in enumerate(VELOCITY):
                    v = grids[(n - 1) % 2][i, x + 1 - cx, pl.ds(8 + 8 * yt - cy, 8), :]
                    f.append(shifted_z(v, cz))
            keep_moments(k, f)

    def relaxation(n, blocks):
        for k, (x, yt) in enumerate(blocks):
            rows = pl.ds(8 + 8 * yt, 8)
            here = pl.ds(8 * yt, 8)
            heat = warm[n, x + 1, rows, :]
            solid = solid_ref[x, here, :] == 1
            g, u = relax_kept(k, heat, solid)
            for i in range(19):
                grids[n % 2][i, x + 1, rows, :] = g[i]
            for d in range(3):
                vel[d, x, here, :] = u[d]

    def heat_block(n, x, yt):
        rows = pl.ds(8 + 8 * yt, 8)
        here = pl.ds(8 * yt, 8)
        centre = warm[n, x + 1, rows, :]
        pairs = (
            (warm[n, x, rows, :], warm[n, x + 2, rows, :]),
            (
                warm[n, x + 1, pl.ds(7 + 8 * yt, 8), :],
                warm[n, x + 1, pl.ds(9 + 8 * yt, 8), :],
            ),
            (shifted_z(centre, 1), shifted_z(centre, -1)),
        )
        laplace = -6.0 * centre
        carried = None
        for d in range(3):
            behind, ahead = pairs[d]
            laplace = laplace + (behind + ahead)
            term = vel[d, x, here, :] * (0.5 * (ahead - behind))
            carried = term if carried is None else carried + term
        solid = solid_ref[x, here, :] == 1
        warm[n + 1, x + 1, rows, :] = jnp.where(solid, centre, centre + diffusion * laplace - carried)

    def send_heat_rows(n):
        ty_send[n, 0] = warm_flat[n, along_x(TOP - 1), :]
        ty_send[n, 1] = warm_flat[n, along_x(LOW + 1), :]

    def take_heat_rows(n):
        warm_flat[n, along_x(LOW), :] = ty_recv[n, 0]
        warm_flat[n, along_x(TOP), :] = ty_recv[n, 1]

    def heat_pass(n):
        copies = t_copies(n)
        wait_recv_all(copies)
        take_heat_rows(n)

        @pl.loop(0, NX)
        def _(x):
            for yt in range(4):
                heat_block(n, x, yt)

        wait_send_all(copies)
        if n < 2:
            send_heat_rows(n + 1)
            start_all(t_copies(n + 1))

    def pack_x(n):
        own = pl.ds(8, NY)
        for k, lane in enumerate(X_UP):
            x_send[n, 0, k] = grids[n % 2][lane, NX, own, :].astype(BF16)
        for k, lane in enumerate(X_DOWN):
            x_send[n, 1, k] = grids[n % 2][lane, 1, own, :].astype(BF16)

    def first_rows(n):
        parts = [(y, half) for y in (NY - 1, 0) for half in range(2)]
        for k, (y, half) in enumerate(parts):
            if n == 0:
                f = [fin_flat[i, pl.ds(8 * half * NY + y, 8, stride=NY), :] for i in range(19)]
            else:
                f = []
                for i, (cx, cy, cz) in enumerate(VELOCITY):
                    rows = along_x(8 + y - cy, 8 * half + 1 - cx, 8)
                    f.append(shifted_z(flats[(n - 1) % 2][i, rows, :], cz))
            keep_moments(4 + k, f)
        for d, lanes in enumerate((Y_UP, Y_DOWN)):
            found = []
            for half in range(2):
                y = parts[2 * d][0]
                heat = warm_flat[n, along_x(8 + y, 8 * half + 1, 8), :]
                solid = solid_flat[pl.ds(8 * half * NY + y, 8, stride=NY), :] == 1
                found.append(relax_kept(4 + 2 * d + half, heat, solid)[0])
            for k, lane in enumerate(lanes):
                both = jnp.concatenate([found[0][lane], found[1][lane]], axis=0)
                y_send[n, d, k] = both.astype(BF16)

    def take_all(n):
        wait_recv_all(x_copies(n))
        own = pl.ds(8, NY)
        for k, lane in enumerate(X_UP):
            grids[n % 2][lane, 0, own, :] = x_recv[n, 0, k].astype(F32)
        for k, lane in enumerate(X_DOWN):
            grids[n % 2][lane, NX + 1, own, :] = x_recv[n, 1, k].astype(F32)
        wait_recv_all(y_copies(n))
        for k, lane in enumerate(Y_UP):
            flats[n % 2][lane, along_x(LOW), :] = y_recv[n, 0, k].astype(F32)
        for k, lane in enumerate(Y_DOWN):
            flats[n % 2][lane, along_x(TOP), :] = y_recv[n, 1, k].astype(F32)
        wait_recv_all(c_copies(n))
        for k, (lane, cx, cy) in enumerate(CORNERS):
            x = 0 if cx > 0 else NX + 1
            y = LOW if cy > 0 else TOP
            row = 7 if cy > 0 else 0
            grids[n % 2][lane, x, pl.ds(y, 1), :] = c_recv[n, k, pl.ds(row, 1), :]

    def border(x):
        return [(x, yt) for yt in range(4)]

    def rim(j):
        return [(1 + 2 * j + k, yt) for k in range(2) for yt in (0, 3)]

    def core_rows(j):
        return [(1 + 2 * j + k, yt) for k in range(2) for yt in (1, 2)]

    last = NX // 2 - 2

    def edges(n):
        if n == 0:
            plane_copy(0).wait()
            plane_copy(NX - 1).wait()
        moments(n, border(0))
        relaxation(n, border(0))
        moments(n, border(NX - 1))
        relaxation(n, border(NX - 1))

    def rims(n):
        moments(n, rim(0))

        @pl.loop(0, last)
        def _(j):
            relaxation(n, rim(j))
            moments(n, rim(j + 1))

        relaxation(n, rim(last))
        moments(n, core_rows(0))

    def middle(n):
        @pl.loop(0, last)
        def _(j):
            relaxation(n, core_rows(j))
            moments(n, core_rows(j + 1))

        relaxation(n, core_rows(last))

    def send_x(n):
        pack_x(n)
        start_all(x_copies(n))
        start_all(c_copies(n))

    def send_y(n):
        first_rows(n)
        start_all(y_copies(n))

    half_cols = 128
    my_half = pl.ds(pl.multiple_of(core * half_cols, half_cols), half_cols)

    def state_copy(d):
        to = lax.rem(slab + d, slabs)
        cols = pl.ds(pl.multiple_of(to * 256 + core * half_cols, half_cols), half_cols)
        return remote(
            state_ref.at[:, cols],
            kept.at[slab, :, my_half],
            hs_sem.at[d],
            hr_sem.at[d],
            (to, tile),
        )

    def partner_copy():
        return remote(
            kept.at[:, :, my_half],
            kept.at[:, :, my_half],
            hs_sem.at[0],
            hr_sem.at[0],
            (slab, partner),
        )

    def start_states():
        for d in range(1, slabs):
            state_copy(d).start()
        mine = pl.ds(pl.multiple_of(slab * 256 + core * half_cols, half_cols), half_cols)
        kept[slab, :, my_half] = state_ref[:, mine]

    def share_states():
        for d in range(1, slabs):
            state_copy(d).wait()
        partner_copy().start()

    def major_copy(d):
        to = lax.rem(s_major + d, majors)
        return remote(
            part.at[pl.ds(2 * to, 2)],
            part_x.at[d - 1],
            pxs_sem.at[d - 1],
            pxr_sem.at[d - 1],
            (2 * to + s_minor, tile),
        )

    def minor_copy():
        return remote(
            pair.at[1 - s_minor],
            part_y,
            pys_sem.at[0],
            pyr_sem.at[0],
            (2 * s_major + 1 - s_minor, tile),
        )

    def multiply():
        partner_copy().wait()
        rows = 2 * RACKS

        def one_pair(m):
            block = kept[pl.ds(2 * m, 2)].reshape(rows, 256)
            column = label_col[pl.ds(pl.multiple_of(m * rows, rows), rows), :]
            total = jnp.zeros((rows, 128), F32)
            for k2 in range(KINDS // 2):
                weights = matrix_ref[pl.ds(2 * k2, 2)].reshape(256, 256)
                product = lax.dot_general(
                    block, weights, (((1,), (1,)), ((), ())), preferred_element_type=F32
                )
                total = jnp.where(column == 2 * k2, product[:, :128], total)
                total = jnp.where(column == 2 * k2 + 1, product[:, 128:], total)
            part[pl.ds(2 * m, 2)] = total.reshape(2, RACKS, 128)

        pl.loop(0, majors)(one_pair)

    def start_majors():
        for d in (2, 1, 3):
            major_copy(d).start()

    def state_rows():
        cols = pl.ds(pl.multiple_of(tile * 128, 128), 128)
        return keep_share * state_ref[:, cols].astype(F32)

    def reduce_major():
        for d in range(1, majors):
            major_copy(d).wait()
        pair[...] = ((part[pl.ds(2 * s_major, 2)] + part_x[0]) + part_x[1]) + part_x[2]
        minor_copy().start()
        own = read_rows[0] * (state_rows() + pair[s_minor])
        other = read_rows[1] * pair[1 - s_minor]
        small_send[pl.ds(1, 1), :] = jnp.sum(jnp.transpose(own), axis=0, keepdims=True)
        row = jnp.sum(jnp.transpose(other), axis=0, keepdims=True)
        cross_send[...] = jnp.broadcast_to(row, (8, 128))

        @pl.loop(0, tiles)
        def _(d):
            cross_copy(d).start()

    def cross_copy(d):
        return remote(
            cross_send,
            cross_recv.at[tile],
            ms_sem.at[1],
            mr_sem.at[1],
            (slab + 1 - 2 * s_minor, lax.rem(tile + d, tiles)),
        )

    def tables():
        for c in table_copies:
            c.wait()
        plan_in[...], tall_in[...] = face_masks(inlet_ref[...], slab, tile, tiles)
        plan_out[...], tall_out[...] = face_masks(outlet_ref[...], slab, tile, tiles)

        @pl.loop(0, slabs)
        def _(b):
            labels = label_ref[pl.ds(b, 1), :]
            rows = pl.ds(pl.multiple_of(b * RACKS, RACKS), RACKS)
            label_col[rows, :] = jnp.transpose(jnp.broadcast_to(labels, (RACKS, 128)))

        cols = pl.ds(pl.multiple_of(tile * 128, 128), 128)
        column = label_col[pl.ds(first_rack, RACKS), :]
        beside = pl.multiple_of((slab + 1 - 2 * s_minor) * RACKS, RACKS)
        column_beside = label_col[pl.ds(beside, RACKS), :]
        gain = jnp.zeros((RACKS, 128), F32)
        read = jnp.zeros((RACKS, 128), F32)
        read_beside = jnp.zeros((RACKS, 128), F32)
        for k in range(KINDS):
            gain = jnp.where(column == k, gain_ref[k : k + 1, cols], gain)
            read = jnp.where(column == k, read_ref[k : k + 1, cols], read)
            read_beside = jnp.where(column_beside == k, read_ref[k : k + 1, cols], read_beside)
        gain_rows[...] = gain
        read_rows[0] = read
        read_rows[1] = read_beside
        per_kind = jnp.sum(gain_ref[...] * read_ref[...], axis=1, keepdims=True)
        kinds = lax.broadcasted_iota(jnp.int32, (KINDS, 128), 0)
        labels = label_ref[pl.ds(slab, 1), :]
        row = jnp.sum(jnp.where(kinds == labels, per_kind, 0.0), axis=0, keepdims=True)
        response[...] = jnp.broadcast_to(row, (8, 128))

    def small_copy(d):
        return remote(
            small_send,
            small_recv.at[d],
            ms_sem.at[0],
            mr_sem.at[0],
            (slab, lax.rem(tile + d, tiles)),
        )

    def small_wait():
        others = small_recv.at[pl.ds(1, tiles - 1)]
        pltpu.make_async_copy(others, others, ms_sem.at[0]).wait()
        pltpu.make_async_copy(others, others, mr_sem.at[0]).wait()
        pltpu.make_async_copy(cross_recv, cross_recv, ms_sem.at[1]).wait()
        pltpu.make_async_copy(cross_recv, cross_recv, mr_sem.at[1]).wait()

    def stream_plane(x):
        for i, (cx, cy, cz) in enumerate(VELOCITY):
            v = grids[0][i, x + 1 - cx, pl.ds(8 - cy, NY), :]
            f_out[i, x] = shifted_z(v, cz)

    solid_copy.wait()

    heat_copy.wait()
    edges(0)
    pl.semaphore_wait(barrier, 2 * (tiles - 1) + (slabs - 1) + 4)
    state_copy_in.wait()
    start_states()
    send_heat_rows(0)
    start_all(t_copies(0))
    send_x(0)

    @pl.loop(1, NX - 1)
    def _(x):
        plane_copy(x).wait()

    send_y(0)
    rims(0)
    middle(0)
    tables()
    share_states()
    heat_pass(0)
    take_all(0)
    wait_send_all(x_copies(0) + y_copies(0) + c_copies(0))

    edges(1)
    send_x(1)
    send_y(1)
    multiply()
    start_majors()
    rims(1)
    middle(1)
    heat_pass(1)
    take_all(1)
    wait_send_all(x_copies(1) + y_copies(1) + c_copies(1))

    edges(2)
    send_x(2)
    send_y(2)
    rims(2)
    reduce_major()
    middle(2)
    heat_pass(2)

    final = warm[3, pl.ds(1, NX), pl.ds(8, NY), :].reshape(NX * NY, NZ)
    sums = jnp.zeros((NX * NY, RACKS), F32)
    for piece in three_parts(final):
        sums = sums + jnp.dot(piece, tall_in[...], preferred_element_type=F32)
    inlet_part = jnp.sum(plan_in[...].astype(F32) * sums, axis=0, keepdims=True)
    small_send[pl.ds(0, 1), :] = inlet_part

    @pl.loop(1, tiles)
    def _(d):
        small_copy(d).start()

    dims = (((1,), (1,)), ((), ()))
    inside = lax.dot_general(plan_out[...], tall_out[...], dims, preferred_element_type=F32)
    final = warm[3, pl.ds(1, NX), pl.ds(8, NY), :].reshape(NX * NY, NZ)
    heat_out[...] = (final - mixing * (inside * final)).reshape(NX, NY, NZ)

    @pl.loop(1, NX - 1)
    def _(x):
        stream_plane(x)

    take_all(2)

    @pl.loop(0, 2)
    def _(j):
        stream_plane(j * (NX - 1))

    out_flat = f_out.reshape(19, NX * NY, NZ)
    for lanes, halo, row in ((Y_UP, LOW, 0), (Y_DOWN, TOP, NY - 1)):
        for lane in lanes:
            cx, _, cz = VELOCITY[lane]
            v = flats[0][lane, along_x(halo, 1 - cx), :]
            out_flat[lane, pl.ds(row, NX, stride=NY), :] = shifted_z(v, cz)

    wait_send_all(x_copies(2) + y_copies(2) + c_copies(2))

    small_wait()
    total = small_send[...]
    for d in range(1, tiles):
        total = total + small_recv[d]
    inlet = total[0:1, :] * (1.0 / FACE)
    readout = total[1:2, :]
    for d in range(tiles):
        readout = readout + cross_recv[d, 0:1, :]
    exhaust = mixing * (readout + response[0:1, :] * inlet)
    spread = jnp.zeros((NX * NY, NZ), F32)
    for piece in three_parts(exhaust):
        spread = spread + lax.dot_general(
            plan_out[...], tall_out[...] * piece, dims, preferred_element_type=F32
        )
    heat_out[...] = heat_out[...] + spread.reshape(NX, NY, NZ)
    inlets = jnp.transpose(jnp.broadcast_to(inlet, (128, RACKS)))
    minor_copy().wait()
    states_out[...] = (state_rows() + (pair[s_minor] + part_y[...])) + gain_rows[...] * inlets


def flush(f_ref, heat_ref, states_ref, f_out, heat_out, states_out, sems):
    copies = [
        pltpu.make_async_copy(heat_ref, heat_out, sems.at[19]),
        pltpu.make_async_copy(states_ref, states_out, sems.at[20]),
    ]
    for i in range(19):
        copies.append(pltpu.make_async_copy(f_ref.at[i], f_out.at[i], sems.at[i]))
    for c in copies:
        c.start()
    for c in copies:
        c.wait()


def per_device(slabs, tiles, f, heat, solid, label, inlet, outlet, matrix, gain, read, state):
    vmem = pl.BlockSpec(memory_space=pltpu.VMEM)
    hbm = pl.BlockSpec(memory_space=pltpu.HBM)
    dma = pltpu.SemaphoreType.DMA
    results = ((19, NX, NY, NZ), (NX, NY, NZ), (RACKS, 128))
    operands = (f, heat, solid, label.reshape(8, 128), inlet.T, outlet.T, matrix, gain, read, state)
    outs = pl.pallas_call(
        functools.partial(kernel, slabs, tiles),
        out_shape=tuple(pltpu.VMEM(shape, F32) for shape in results),
        in_specs=[hbm] * 10,
        out_specs=(vmem, vmem, vmem),
        scratch_shapes=[
            pltpu.VMEM((19, NX, NY, NZ), F32),
            pltpu.VMEM((19, NX + 2, ROWS, NZ), F32),
            pltpu.VMEM((19, NX + 2, ROWS, NZ), F32),
            pltpu.VMEM((4, NX + 2, ROWS, NZ), F32),
            pltpu.VMEM((3, NX, NY, NZ), F32),
            pltpu.VMEM((8, 23, 8, NZ), F32),
            pltpu.VMEM((NX, NY, NZ), jnp.int32),
            pltpu.VMEM((FACE, RACKS), jnp.int32),
            pltpu.VMEM((FACE, RACKS), jnp.int32),
            pltpu.VMEM((slabs, 128), jnp.int32),
            pltpu.VMEM((KINDS, 128, 256), BF16),
            pltpu.VMEM((KINDS, tiles * 128), F32),
            pltpu.VMEM((KINDS, tiles * 128), F32),
            pltpu.VMEM((RACKS, tiles * 128), BF16),
            pltpu.VMEM((3, 2, 5, NY, NZ), BF16),
            pltpu.VMEM((3, 2, 5, NY, NZ), BF16),
            pltpu.VMEM((3, 2, 5, NX, NZ), BF16),
            pltpu.VMEM((3, 2, 5, NX, NZ), BF16),
            pltpu.VMEM((3, 4, 8, NZ), F32),
            pltpu.VMEM((3, 2, NX, NZ), F32),
            pltpu.VMEM((3, 2, NX, NZ), F32),
            pltpu.VMEM((slabs, RACKS, 256), BF16),
            pltpu.VMEM((slabs * RACKS, 128), jnp.int32),
            pltpu.VMEM((NX * NY, RACKS), BF16),
            pltpu.VMEM((NZ, RACKS), BF16),
            pltpu.VMEM((NX * NY, RACKS), BF16),
            pltpu.VMEM((NZ, RACKS), BF16),
            pltpu.VMEM((RACKS, 128), F32),
            pltpu.VMEM((2, RACKS, 128), F32),
            pltpu.VMEM((8, 128), F32),
            pltpu.VMEM((slabs, RACKS, 128), F32),
            pltpu.VMEM((slabs // 2 - 1, 2, RACKS, 128), F32),
            pltpu.VMEM((2, RACKS, 128), F32),
            pltpu.VMEM((RACKS, 128), F32),
            pltpu.VMEM((8, 128), F32),
            pltpu.VMEM((tiles, 8, 128), F32),
            pltpu.VMEM((8, 128), F32),
            pltpu.VMEM((tiles, 8, 128), F32),
            dma((NX,)),
            dma((1,)),
            dma((8,)),
            dma((3, 2)),
            dma((3, 2)),
            dma((3, 2)),
            dma((3, 2)),
            dma((3, 4)),
            dma((3, 4)),
            dma((3, 4)),
            dma((3, 4)),
            dma((slabs,)),
            dma((slabs,)),
            dma((3,)),
            dma((3,)),
            dma((1,)),
            dma((1,)),
            dma((2,)),
            dma((2,)),
        ],
        compiler_params=pltpu.CompilerParams(
            collective_id=0, has_side_effects=True, vmem_limit_bytes=40 * 1024 * 1024
        ),
    )(*(pltpu.with_memory_space_constraint(a, pltpu.HBM) for a in operands))
    return pl.pallas_call(
        flush,
        out_shape=tuple(jax.ShapeDtypeStruct(shape, F32) for shape in results),
        in_specs=[vmem] * 3,
        out_specs=(hbm,) * 3,
        scratch_shapes=[dma((21,))],
        compiler_params=pltpu.CompilerParams(vmem_limit_bytes=1024 * 1024),
    )(*outs)


def solution(mesh):
    slabs, tiles = mesh.shape["slab"], mesh.shape["tile"]
    return jax.shard_map(
        functools.partial(per_device, slabs, tiles),
        mesh=mesh,
        in_specs=(
            P(None, "slab", "tile", None),
            P("slab", "tile", None),
            P("slab", "tile", None),
            P(),
            P(),
            P(),
            P(None, "tile", "slab"),
            P(),
            P(),
            P("slab", None),
        ),
        out_specs=(P(None, "slab", "tile", None), P("slab", "tile", None), P("slab", "tile")),
        check_vma=False,
    )
```

```python
import functools

import jax
import jax.numpy as jnp
from jax import lax
from jax.experimental import pallas as pl
from jax.experimental.pallas import tpu as pltpu
from jax.sharding import PartitionSpec as P

MESH = pl.DeviceIdType.MESH
F32 = jnp.float32
BF16 = jnp.bfloat16

VELOCITY = (
    (0, 0, 0),
    (1, 0, 0),
    (-1, 0, 0),
    (0, 1, 0),
    (0, -1, 0),
    (0, 0, 1),
    (0, 0, -1),
    (1, 1, 0),
    (-1, -1, 0),
    (1, -1, 0),
    (-1, 1, 0),
    (1, 0, 1),
    (-1, 0, -1),
    (1, 0, -1),
    (-1, 0, 1),
    (0, 1, 1),
    (0, -1, -1),
    (0, 1, -1),
    (0, -1, 1),
)
X_UP = (1, 7, 9, 11, 13)
X_DOWN = (2, 8, 10, 12, 14)
Y_UP = (3, 7, 10, 15, 17)
Y_DOWN = (4, 8, 9, 16, 18)
CORNERS = ((7, 1, 1), (8, -1, -1), (9, 1, -1), (10, -1, 1))

relax_time = 0.6
buoyancy = 0.01
diffusion = 0.1
mixing = 0.5
keep_share = 0.5

NX, NY, NZ = 16, 32, 128
ROWS = 48
LOW, TOP = 7, 40
KINDS = 8
RACKS = 128
FACE = 32


def gather_moments(f):
    even = [f[p] + f[p + 1] for p in range(1, 19, 2)]
    odd = [f[p] - f[p + 1] for p in range(1, 19, 2)]
    density = (
        f[0]
        + ((even[0] + even[1]) + (even[2] + even[3]))
        + ((even[4] + even[5]) + (even[6] + even[7]))
        + even[8]
    )
    flow_x = (odd[0] + odd[3]) + (odd[4] + odd[5]) + odd[6]
    flow_y = (odd[1] + odd[3]) + (odd[7] - odd[4]) + odd[8]
    flow_z = (odd[2] + odd[5]) + (odd[7] - odd[6]) - odd[8]
    return f[0], even, odd, density, flow_x, flow_y, flow_z


def relax(still, even, odd, density, flow_x, flow_y, flow_z, heat, solid):
    omega = 1.0 / relax_time
    keep = 1.0 - omega
    inverse = jnp.where(solid, 0.0, 1.0 / density)
    share = jnp.where(solid, 0.0, density * (omega / 18.0))
    even_part = jnp.where(solid, 0.5, 0.5 * keep)
    odd_part = jnp.where(solid, -0.5, 0.5 * keep)
    ux = flow_x * inverse
    uy = flow_y * inverse
    uz = flow_z * inverse
    vz = (flow_z + (relax_time * buoyancy) * heat) * inverse
    bend = share * 4.5
    lean = share * 3.0
    ex, ey, ez = bend * ux, bend * uy, bend * vz
    xx, yy, zz = ex * ux, ey * uy, ez * vz
    level = share - (xx + yy + zz) * (1.0 / 3.0)
    sx, sy, sz = level + xx, level + yy, level + zz
    tx, ty, tz = lean * ux, lean * uy, lean * vz
    hx, hy, hz = 0.5 * tx, 0.5 * ty, 0.5 * tz
    mxy, mxz, myz = 0.5 * (sx + yy), 0.5 * (sx + zz), 0.5 * (sy + zz)
    qxy, qxz, qyz = ex * uy, ex * vz, ey * vz
    terms = {
        1: (sx, tx),
        3: (sy, ty),
        5: (sz, tz),
        7: (mxy + qxy, hx + hy),
        9: (mxy - qxy, hx - hy),
        11: (mxz + qxz, hx + hz),
        13: (mxz - qxz, hx - hz),
        15: (myz + qyz, hy + hz),
        17: (myz - qyz, hy - hz),
    }
    g = [None] * 19
    g[0] = still * jnp.where(solid, 1.0, keep) + level * 6.0
    for p in range(1, 19, 2):
        same, turn = terms[p]
        both = even[p // 2] * even_part + same
        half = odd[p // 2] * odd_part + turn
        g[p] = both + half
        g[p + 1] = both - half
    return g, (ux, uy, uz)


def shifted_z(v, step):
    return pltpu.roll(v, step % NZ, 1) if step else v


def face_masks(pos, slab, tile, tiles):
    height_bits = NZ.bit_length() - 1
    across = NY * tiles
    across_bits = across.bit_length() - 1
    px = jnp.right_shift(pos, height_bits + across_bits)
    py = jnp.bitwise_and(jnp.right_shift(pos, height_bits), across - 1)
    pz = jnp.bitwise_and(pos, NZ - 1)
    least = functools.partial(jnp.min, axis=0, keepdims=True)
    x0, y0, z0 = least(px), least(py), least(pz)
    y1 = jnp.max(py, axis=0, keepdims=True)
    lifted = least(py + jnp.where(py < across // 2, across, 0))
    y0 = jnp.where(y1 - y0 > 3, lifted, y0)
    row = lax.broadcasted_iota(jnp.int32, (NX * NY, RACKS), 0)
    gx = slab * NX + jnp.right_shift(row, 5)
    gy = tile * NY + jnp.bitwise_and(row, NY - 1)
    off_y = jnp.bitwise_and(gy - y0, across - 1)
    plan = jnp.where((gx == x0) & (off_y < 4), 1.0, 0.0).astype(BF16)
    z = lax.broadcasted_iota(jnp.int32, (NZ, RACKS), 0)
    tall = jnp.where((z >= z0) & (z < z0 + 8), 1.0, 0.0).astype(BF16)
    return plan, tall


def three_parts(v):
    a = v.astype(BF16)
    rest = v - a.astype(F32)
    b = rest.astype(BF16)
    return a, b, (rest - b.astype(F32)).astype(BF16)


def kernel(
    slabs,
    tiles,
    f_hbm,
    heat_hbm,
    solid_hbm,
    label_hbm,
    inlet_hbm,
    outlet_hbm,
    matrix_hbm,
    gain_hbm,
    read_hbm,
    state_hbm,
    f_out,
    heat_out,
    states_out,
    fin,
    grid_even,
    grid_odd,
    warm,
    vel,
    mid,
    mid_all,
    solid_ref,
    inlet_ref,
    outlet_ref,
    label_ref,
    matrix_ref,
    gain_ref,
    read_ref,
    state_ref,
    x_send,
    x_recv,
    y_send,
    y_recv,
    c_recv,
    ty_send,
    ty_recv,
    stage,
    kept,
    label_col,
    plan_in,
    tall_in,
    plan_out,
    tall_out,
    gain_rows,
    read_rows,
    response,
    part,
    part_x,
    pair,
    part_y,
    cross_send,
    cross_recv,
    small_send,
    small_recv,
    load_sem,
    heat_sem,
    misc_sem,
    xs_sem,
    xr_sem,
    ys_sem,
    yr_sem,
    cs_sem,
    cr_sem,
    tsend_sem,
    trecv_sem,
    hs_sem,
    hr_sem,
    pxs_sem,
    pxr_sem,
    pys_sem,
    pyr_sem,
    ms_sem,
    mr_sem,
):
    grids = (grid_even, grid_odd)
    flats = [g.reshape(19, (NX + 2) * ROWS, NZ) for g in grids]
    warm_flat = warm.reshape(4, (NX + 2) * ROWS, NZ)
    fin_flat = fin.reshape(19, NX * NY, NZ)
    solid_flat = solid_ref.reshape(NX * NY, NZ)

    def along_x(row, first=1, count=NX):
        return pl.ds(first * ROWS + row, count, stride=ROWS)

    slab = lax.axis_index("slab")
    tile = lax.axis_index("tile")
    s_up, s_down = lax.rem(slab + 1, slabs), lax.rem(slab + slabs - 1, slabs)
    t_up, t_down = lax.rem(tile + 1, tiles), lax.rem(tile + tiles - 1, tiles)
    core = lax.rem(tile, 2)
    partner = tile + 1 - 2 * core
    s_major = slab // 2
    s_minor = lax.rem(slab, 2)
    majors = slabs // 2

    def plane_copy(x):
        return pltpu.make_async_copy(f_hbm.at[:, x], fin.at[:, x], load_sem.at[x])

    heat_copy = pltpu.make_async_copy(
        heat_hbm, warm.at[0, pl.ds(1, NX), pl.ds(8, NY), :], heat_sem.at[0]
    )

    solid_copy = pltpu.make_async_copy(solid_hbm, solid_ref, misc_sem.at[0])
    first_rack = pl.multiple_of(slab * RACKS, RACKS)
    inlet_copy = pltpu.make_async_copy(
        inlet_hbm.at[:, pl.ds(first_rack, RACKS)], inlet_ref, misc_sem.at[1]
    )
    outlet_copy = pltpu.make_async_copy(
        outlet_hbm.at[:, pl.ds(first_rack, RACKS)], outlet_ref, misc_sem.at[2]
    )
    solid_copy.start()

    heat_copy.start()
    plane_copy(0).start()
    plane_copy(NX - 1).start()
    state_copy_in = pltpu.make_async_copy(state_hbm, state_ref, misc_sem.at[7])
    state_copy_in.start()

    label_copy = pltpu.make_async_copy(label_hbm, label_ref, misc_sem.at[3])
    matrix_copy = pltpu.make_async_copy(matrix_hbm, matrix_ref, misc_sem.at[4])
    gain_copy = pltpu.make_async_copy(gain_hbm, gain_ref, misc_sem.at[5])
    read_copy = pltpu.make_async_copy(read_hbm, read_ref, misc_sem.at[6])
    table_copies = (label_copy, inlet_copy, outlet_copy, gain_copy, read_copy, matrix_copy)

    barrier = pltpu.get_barrier_semaphore()

    @pl.loop(1, tiles)
    def _(d):
        pl.semaphore_signal(
            barrier, inc=1, device_id=(slab, lax.rem(tile + d, tiles)), device_id_type=MESH
        )

    @pl.loop(1, slabs)
    def _(d):
        pl.semaphore_signal(
            barrier, inc=1, device_id=(lax.rem(slab + d, slabs), tile), device_id_type=MESH
        )

    @pl.loop(1, tiles)
    def _(d):
        to = (slab + 1 - 2 * s_minor, lax.rem(tile + d, tiles))
        pl.semaphore_signal(barrier, inc=1, device_id=to, device_id_type=MESH)

    for ds in (s_up, s_down):
        for dt in (t_up, t_down):
            pl.semaphore_signal(barrier, inc=1, device_id=(ds, dt), device_id_type=MESH)

    def remote(src, dst, send, recv, to):
        return pltpu.make_async_remote_copy(
            src_ref=src,
            dst_ref=dst,
            send_sem=send,
            recv_sem=recv,
            device_id=to,
            device_id_type=MESH,
        )

    def x_copies(n):
        return [
            remote(x_send.at[n, 0], x_recv.at[n, 0], xs_sem.at[n, 0], xr_sem.at[n, 0], (s_up, tile)),
            remote(x_send.at[n, 1], x_recv.at[n, 1], xs_sem.at[n, 1], xr_sem.at[n, 1], (s_down, tile)),
        ]

    def y_copies(n):
        return [
            remote(y_send.at[n, 0], y_recv.at[n, 0], ys_sem.at[n, 0], yr_sem.at[n, 0], (slab, t_up)),
            remote(y_send.at[n, 1], y_recv.at[n, 1], ys_sem.at[n, 1], yr_sem.at[n, 1], (slab, t_down)),
        ]

    def c_copies(n):
        out = []
        for k, (lane, cx, cy) in enumerate(CORNERS):
            x = NX if cx > 0 else 1
            y = TOP - 8 if cy > 0 else LOW + 1
            to = (s_up if cx > 0 else s_down, t_up if cy > 0 else t_down)
            out.append(
                remote(
                    grids[n % 2].at[lane, x, pl.ds(y, 8), :],
                    c_recv.at[n, k],
                    cs_sem.at[n, k],
                    cr_sem.at[n, k],
                    to,
                )
            )
        return out

    def t_copies(n):
        own = pl.ds(8, NY)
        return [
            remote(
                warm.at[n, NX, own, :],
                warm.at[n, 0, own, :],
                tsend_sem.at[n, 0],
                trecv_sem.at[n, 0],
                (s_up, tile),
            ),
            remote(
                warm.at[n, 1, own, :],
                warm.at[n, NX + 1, own, :],
                tsend_sem.at[n, 1],
                trecv_sem.at[n, 1],
                (s_down, tile),
            ),
            remote(ty_send.at[n, 0], ty_recv.at[n, 0], tsend_sem.at[n, 2], trecv_sem.at[n, 2], (slab, t_up)),
            remote(ty_send.at[n, 1], ty_recv.at[n, 1], tsend_sem.at[n, 3], trecv_sem.at[n, 3], (slab, t_down)),
        ]

    def start_all(copies):
        for c in copies:
            c.start()

    def wait_recv_all(copies):
        for c in copies:
            c.wait_recv()

    def wait_send_all(copies):
        for c in copies:
            c.wait_send()

    def keep_moments(slot, f, store=mid):
        still, even, odd, density, *flow = gather_moments(f)
        for i, v in enumerate((still, density, *flow, *even, *odd)):
            store[slot, i] = v
        return density, flow

    def relax_kept(slot, heat, solid, store=mid):
        even = [store[slot, 5 + i] for i in range(9)]
        odd = [store[slot, 14 + i] for i in range(9)]
        still, density, *flow = [store[slot, i] for i in range(5)]
        return relax(still, even, odd, density, *flow, heat, solid)

    def moments(n, blocks):
        for k, (x, yt) in enumerate(blocks):
            here = pl.ds(8 * yt, 8)
            if n == 0:
                f = [fin[i, x, here, :] for i in range(19)]
            else:
                f = []
                for i, (cx, cy, cz) in enumerate(VELOCITY):
                    v = grids[(n - 1) % 2][i, x + 1 - cx, pl.ds(8 + 8 * yt - cy, 8), :]
                    f.append(shifted_z(v, cz))
            keep_moments(k, f)

    def relaxation(n, blocks):
        for k, (x, yt) in enumerate(blocks):
            rows = pl.ds(8 + 8 * yt, 8)
            here = pl.ds(8 * yt, 8)
            heat = warm[n, x + 1, rows, :]
            solid = solid_ref[x, here, :] == 1
            g, u = relax_kept(k, heat, solid)
            for i in range(19):
                grids[n % 2][i, x + 1, rows, :] = g[i]
            for d in range(3):
                vel[d, x, here, :] = u[d]

    def heat_block(n, x, yt):
        rows = pl.ds(8 + 8 * yt, 8)
        here = pl.ds(8 * yt, 8)
        centre = warm[n, x + 1, rows, :]
        pairs = (
            (warm[n, x, rows, :], warm[n, x + 2, rows, :]),
            (
                warm[n, x + 1, pl.ds(7 + 8 * yt, 8), :],
                warm[n, x + 1, pl.ds(9 + 8 * yt, 8), :],
            ),
            (shifted_z(centre, 1), shifted_z(centre, -1)),
        )
        laplace = -6.0 * centre
        carried = None
        for d in range(3):
            behind, ahead = pairs[d]
            laplace = laplace + (behind + ahead)
            term = vel[d, x, here, :] * (0.5 * (ahead - behind))
            carried = term if carried is None else carried + term
        solid = solid_ref[x, here, :] == 1
        warm[n + 1, x + 1, rows, :] = jnp.where(solid, centre, centre + diffusion * laplace - carried)

    def send_heat_rows(n):
        ty_send[n, 0] = warm_flat[n, along_x(TOP - 1), :]
        ty_send[n, 1] = warm_flat[n, along_x(LOW + 1), :]

    def take_heat_rows(n):
        warm_flat[n, along_x(LOW), :] = ty_recv[n, 0]
        warm_flat[n, along_x(TOP), :] = ty_recv[n, 1]

    def heat_pass(n):
        copies = t_copies(n)
        wait_recv_all(copies)
        take_heat_rows(n)

        @pl.loop(0, NX)
        def _(x):
            for yt in range(4):
                heat_block(n, x, yt)

        wait_send_all(copies)
        if n < 2:
            send_heat_rows(n + 1)
            start_all(t_copies(n + 1))

    def pack_x(n):
        own = pl.ds(8, NY)
        for k, lane in enumerate(X_UP):
            x_send[n, 0, k] = grids[n % 2][lane, NX, own, :].astype(BF16)
        for k, lane in enumerate(X_DOWN):
            x_send[n, 1, k] = grids[n % 2][lane, 1, own, :].astype(BF16)

    def first_rows(n):
        parts = [(y, half) for y in (NY - 1, 0) for half in range(2)]
        for k, (y, half) in enumerate(parts):
            if n == 0:
                f = [fin_flat[i, pl.ds(8 * half * NY + y, 8, stride=NY), :] for i in range(19)]
            else:
                f = []
                for i, (cx, cy, cz) in enumerate(VELOCITY):
                    rows = along_x(8 + y - cy, 8 * half + 1 - cx, 8)
                    f.append(shifted_z(flats[(n - 1) % 2][i, rows, :], cz))
            keep_moments(4 + k, f)
        for d, lanes in enumerate((Y_UP, Y_DOWN)):
            found = []
            for half in range(2):
                y = parts[2 * d][0]
                heat = warm_flat[n, along_x(8 + y, 8 * half + 1, 8), :]
                solid = solid_flat[pl.ds(8 * half * NY + y, 8, stride=NY), :] == 1
                found.append(relax_kept(4 + 2 * d + half, heat, solid)[0])
            for k, lane in enumerate(lanes):
                both = jnp.concatenate([found[0][lane], found[1][lane]], axis=0)
                y_send[n, d, k] = both.astype(BF16)

    def take_all(n):
        wait_recv_all(x_copies(n))
        own = pl.ds(8, NY)
        for k, lane in enumerate(X_UP):
            grids[n % 2][lane, 0, own, :] = x_recv[n, 0, k].astype(F32)
        for k, lane in enumerate(X_DOWN):
            grids[n % 2][lane, NX + 1, own, :] = x_recv[n, 1, k].astype(F32)
        wait_recv_all(y_copies(n))
        for k, lane in enumerate(Y_UP):
            flats[n % 2][lane, along_x(LOW), :] = y_recv[n, 0, k].astype(F32)
        for k, lane in enumerate(Y_DOWN):
            flats[n % 2][lane, along_x(TOP), :] = y_recv[n, 1, k].astype(F32)
        wait_recv_all(c_copies(n))
        for k, (lane, cx, cy) in enumerate(CORNERS):
            x = 0 if cx > 0 else NX + 1
            y = LOW if cy > 0 else TOP
            row = 7 if cy > 0 else 0
            grids[n % 2][lane, x, pl.ds(y, 1), :] = c_recv[n, k, pl.ds(row, 1), :]

    def border(x):
        return [(x, yt) for yt in range(4)]

    def rim(j):
        return [(1 + 2 * j + k, yt) for k in range(2) for yt in (0, 3)]

    def core_rows(j):
        return [(1 + 2 * j + k, yt) for k in range(2) for yt in (1, 2)]

    last = NX // 2 - 2

    def edges(n):
        if n == 0:
            plane_copy(0).wait()
            plane_copy(NX - 1).wait()

            @pl.loop(1, NX - 1)
            def _(x):
                plane_copy(x).start()

            for c in table_copies:
                c.start()
        moments(n, border(0))
        relaxation(n, border(0))
        moments(n, border(NX - 1))
        relaxation(n, border(NX - 1))

    def rims(n):
        moments(n, rim(0))

        @pl.loop(0, last)
        def _(j):
            relaxation(n, rim(j))
            moments(n, rim(j + 1))

        relaxation(n, rim(last))
        moments(n, core_rows(0))

    def middle(n):
        @pl.loop(0, last)
        def _(j):
            relaxation(n, core_rows(j))
            moments(n, core_rows(j + 1))

        relaxation(n, core_rows(last))

    def inner_moments(n):
        @pl.loop(0, last + 1)
        def _(j):
            for k, (x, yt) in enumerate(rim(j) + core_rows(j)):
                f = []
                for i, (cx, cy, cz) in enumerate(VELOCITY):
                    v = grids[(n - 1) % 2][i, x + 1 - cx, pl.ds(8 + 8 * yt - cy, 8), :]
                    f.append(shifted_z(v, cz))
                density, flow = keep_moments(8 * j + k, f, mid_all)
                solid = solid_ref[x, pl.ds(8 * yt, 8), :] == 1
                inverse = jnp.where(solid, 0.0, 1.0 / density)
                for d in range(3):
                    vel[d, x, pl.ds(8 * yt, 8), :] = flow[d] * inverse

    def inner_relaxation(n):
        @pl.loop(0, last + 1)
        def _(j):
            for k, (x, yt) in enumerate(rim(j) + core_rows(j)):
                rows = pl.ds(8 + 8 * yt, 8)
                heat = warm[n, x + 1, rows, :]
                solid = solid_ref[x, pl.ds(8 * yt, 8), :] == 1
                g, _ = relax_kept(8 * j + k, heat, solid, mid_all)
                for i in range(19):
                    grids[n % 2][i, x + 1, rows, :] = g[i]

    def send_x(n):
        pack_x(n)
        start_all(x_copies(n))
        start_all(c_copies(n))

    def send_y(n):
        first_rows(n)
        start_all(y_copies(n))

    half_cols = 128

    def state_copy(d):
        to = lax.rem(slab + d, slabs)
        return remote(
            stage.at[to], kept.at[core, slab], hs_sem.at[d], hr_sem.at[d], (to, tile)
        )

    def partner_copy():
        return remote(
            kept.at[core], kept.at[core], hs_sem.at[0], hr_sem.at[0], (slab, partner)
        )

    def start_states():
        for b in range(slabs):
            cols = pl.ds(pl.multiple_of(b * 256 + core * half_cols, half_cols), half_cols)
            stage[b] = state_ref[:, cols]
        for d in range(1, slabs):
            state_copy(d).start()
        kept[core, slab] = stage[slab]

    def share_states():
        for d in range(1, slabs):
            state_copy(d).wait()
        partner_copy().start()

    def major_copy(d):
        to = lax.rem(s_major + d, majors)
        return remote(
            part.at[pl.ds(2 * to, 2)],
            part_x.at[d - 1],
            pxs_sem.at[d - 1],
            pxr_sem.at[d - 1],
            (2 * to + s_minor, tile),
        )

    def minor_copy():
        return remote(
            pair.at[1 - s_minor],
            part_y,
            pys_sem.at[0],
            pyr_sem.at[0],
            (2 * s_major + 1 - s_minor, tile),
        )

    def multiply():
        partner_copy().wait()
        rows = 2 * RACKS

        def one_pair(m):
            block = jnp.concatenate(
                [kept[c, pl.ds(2 * m, 2)].reshape(rows, 128) for c in range(2)], axis=1
            )
            column = label_col[pl.ds(pl.multiple_of(m * rows, rows), rows), :]
            total = jnp.zeros((rows, 128), F32)
            for k2 in range(KINDS // 2):
                weights = matrix_ref[pl.ds(2 * k2, 2)].reshape(256, 256)
                product = lax.dot_general(
                    block, weights, (((1,), (1,)), ((), ())), preferred_element_type=F32
                )
                total = jnp.where(column == 2 * k2, product[:, :128], total)
                total = jnp.where(column == 2 * k2 + 1, product[:, 128:], total)
            part[pl.ds(2 * m, 2)] = total.reshape(2, RACKS, 128)

        @pl.loop(0, majors - 1)
        def _(j):
            d = jnp.where(j == 0, 2, jnp.where(j == 1, 1, 3))
            one_pair(lax.rem(s_major + d, majors))
            major_copy(d).start()

        one_pair(s_major)

    def state_rows():
        cols = pl.ds(pl.multiple_of(tile * 128, 128), 128)
        return keep_share * state_ref[:, cols].astype(F32)

    def reduce_major():
        for d in range(1, majors):
            major_copy(d).wait()
        pair[...] = ((part[pl.ds(2 * s_major, 2)] + part_x[0]) + part_x[1]) + part_x[2]
        minor_copy().start()
        own = read_rows[0] * (state_rows() + pair[s_minor])
        other = read_rows[1] * pair[1 - s_minor]
        small_send[pl.ds(1, 1), :] = jnp.sum(jnp.transpose(own), axis=0, keepdims=True)
        row = jnp.sum(jnp.transpose(other), axis=0, keepdims=True)
        cross_send[...] = jnp.broadcast_to(row, (8, 128))

        @pl.loop(0, tiles)
        def _(d):
            cross_copy(d).start()

    def cross_copy(d):
        return remote(
            cross_send,
            cross_recv.at[tile],
            ms_sem.at[1],
            mr_sem.at[1],
            (slab + 1 - 2 * s_minor, lax.rem(tile + d, tiles)),
        )

    def tables():
        for c in table_copies:
            c.wait()
        plan_in[...], tall_in[...] = face_masks(inlet_ref[...], slab, tile, tiles)
        plan_out[...], tall_out[...] = face_masks(outlet_ref[...], slab, tile, tiles)

        @pl.loop(0, slabs)
        def _(b):
            labels = label_ref[pl.ds(b, 1), :]
            rows = pl.ds(pl.multiple_of(b * RACKS, RACKS), RACKS)
            label_col[rows, :] = jnp.transpose(jnp.broadcast_to(labels, (RACKS, 128)))

        cols = pl.ds(pl.multiple_of(tile * 128, 128), 128)
        column = label_col[pl.ds(first_rack, RACKS), :]
        beside = pl.multiple_of((slab + 1 - 2 * s_minor) * RACKS, RACKS)
        column_beside = label_col[pl.ds(beside, RACKS), :]
        gain = jnp.zeros((RACKS, 128), F32)
        read = jnp.zeros((RACKS, 128), F32)
        read_beside = jnp.zeros((RACKS, 128), F32)
        for k in range(KINDS):
            gain = jnp.where(column == k, gain_ref[k : k + 1, cols], gain)
            read = jnp.where(column == k, read_ref[k : k + 1, cols], read)
            read_beside = jnp.where(column_beside == k, read_ref[k : k + 1, cols], read_beside)
        gain_rows[...] = gain
        read_rows[0] = read
        read_rows[1] = read_beside
        per_kind = jnp.sum(gain_ref[...] * read_ref[...], axis=1, keepdims=True)
        kinds = lax.broadcasted_iota(jnp.int32, (KINDS, 128), 0)
        labels = label_ref[pl.ds(slab, 1), :]
        row = jnp.sum(jnp.where(kinds == labels, per_kind, 0.0), axis=0, keepdims=True)
        response[...] = jnp.broadcast_to(row, (8, 128))

    def small_copy(d):
        return remote(
            small_send,
            small_recv.at[d],
            ms_sem.at[0],
            mr_sem.at[0],
            (slab, lax.rem(tile + d, tiles)),
        )

    def small_wait():
        others = small_recv.at[pl.ds(1, tiles - 1)]
        pltpu.make_async_copy(others, others, ms_sem.at[0]).wait()
        pltpu.make_async_copy(others, others, mr_sem.at[0]).wait()
        pltpu.make_async_copy(cross_recv, cross_recv, ms_sem.at[1]).wait()
        pltpu.make_async_copy(cross_recv, cross_recv, mr_sem.at[1]).wait()

    def stream_plane(x):
        for i, (cx, cy, cz) in enumerate(VELOCITY):
            v = grids[0][i, x + 1 - cx, pl.ds(8 - cy, NY), :]
            f_out[i, x] = shifted_z(v, cz)

    solid_copy.wait()

    heat_copy.wait()
    edges(0)
    pl.semaphore_wait(barrier, 2 * (tiles - 1) + (slabs - 1) + 4)
    state_copy_in.wait()
    start_states()
    send_heat_rows(0)
    start_all(t_copies(0))
    send_x(0)

    @pl.loop(1, NX - 1)
    def _(x):
        plane_copy(x).wait()

    send_y(0)
    rims(0)
    middle(0)
    tables()
    share_states()
    heat_pass(0)
    take_all(0)
    wait_send_all(x_copies(0) + y_copies(0) + c_copies(0))

    edges(1)
    send_x(1)
    send_y(1)
    multiply()
    rims(1)
    middle(1)
    heat_pass(1)
    take_all(1)
    wait_send_all(x_copies(1) + y_copies(1) + c_copies(1))

    edges(2)
    send_x(2)
    send_y(2)
    inner_moments(2)
    reduce_major()
    heat_pass(2)

    final = warm[3, pl.ds(1, NX), pl.ds(8, NY), :].reshape(NX * NY, NZ)
    sums = jnp.dot(
        jnp.concatenate(three_parts(final), axis=1),
        jnp.concatenate([tall_in[...]] * 3, axis=0),
        preferred_element_type=F32,
    )
    inlet_part = jnp.sum(plan_in[...].astype(F32) * sums, axis=0, keepdims=True)
    small_send[pl.ds(0, 1), :] = inlet_part

    @pl.loop(1, tiles)
    def _(d):
        small_copy(d).start()

    inner_relaxation(2)

    dims = (((1,), (1,)), ((), ()))
    inside = lax.dot_general(plan_out[...], tall_out[...], dims, preferred_element_type=F32)
    final = warm[3, pl.ds(1, NX), pl.ds(8, NY), :].reshape(NX * NY, NZ)
    heat_out[...] = (final - mixing * (inside * final)).reshape(NX, NY, NZ)

    @pl.loop(1, NX - 1)
    def _(x):
        stream_plane(x)

    take_all(2)

    @pl.loop(0, 2)
    def _(j):
        stream_plane(j * (NX - 1))

    out_flat = f_out.reshape(19, NX * NY, NZ)
    for lanes, halo, row in ((Y_UP, LOW, 0), (Y_DOWN, TOP, NY - 1)):
        for lane in lanes:
            cx, _, cz = VELOCITY[lane]
            v = flats[0][lane, along_x(halo, 1 - cx), :]
            out_flat[lane, pl.ds(row, NX, stride=NY), :] = shifted_z(v, cz)

    wait_send_all(x_copies(2) + y_copies(2) + c_copies(2))

    small_wait()
    total = small_send[...]
    for d in range(1, tiles):
        total = total + small_recv[d]
    inlet = total[0:1, :] * (1.0 / FACE)
    readout = total[1:2, :]
    for d in range(tiles):
        readout = readout + cross_recv[d, 0:1, :]
    exhaust = mixing * (readout + response[0:1, :] * inlet)
    spread = lax.dot_general(
        jnp.concatenate([plan_out[...]] * 3, axis=1),
        jnp.concatenate([tall_out[...] * piece for piece in three_parts(exhaust)], axis=1),
        dims,
        preferred_element_type=F32,
    )
    heat_out[...] = heat_out[...] + spread.reshape(NX, NY, NZ)
    inlets = jnp.transpose(jnp.broadcast_to(inlet, (128, RACKS)))
    minor_copy().wait()
    states_out[...] = (state_rows() + (pair[s_minor] + part_y[...])) + gain_rows[...] * inlets


def flush(f_ref, heat_ref, states_ref, f_out, heat_out, states_out, sems):
    copies = [
        pltpu.make_async_copy(heat_ref, heat_out, sems.at[19]),
        pltpu.make_async_copy(states_ref, states_out, sems.at[20]),
    ]
    for i in range(19):
        copies.append(pltpu.make_async_copy(f_ref.at[i], f_out.at[i], sems.at[i]))
    for c in copies:
        c.start()
    for c in copies:
        c.wait()


def per_device(slabs, tiles, f, heat, solid, label, inlet, outlet, matrix, gain, read, state):
    vmem = pl.BlockSpec(memory_space=pltpu.VMEM)
    hbm = pl.BlockSpec(memory_space=pltpu.HBM)
    dma = pltpu.SemaphoreType.DMA
    results = ((19, NX, NY, NZ), (NX, NY, NZ), (RACKS, 128))
    operands = (f, heat, solid, label.reshape(8, 128), inlet.T, outlet.T, matrix, gain, read, state)
    outs = pl.pallas_call(
        functools.partial(kernel, slabs, tiles),
        out_shape=tuple(pltpu.VMEM(shape, F32) for shape in results),
        in_specs=[hbm] * 10,
        out_specs=(vmem, vmem, vmem),
        scratch_shapes=[
            pltpu.VMEM((19, NX, NY, NZ), F32),
            pltpu.VMEM((19, NX + 2, ROWS, NZ), F32),
            pltpu.VMEM((19, NX + 2, ROWS, NZ), F32),
            pltpu.VMEM((4, NX + 2, ROWS, NZ), F32),
            pltpu.VMEM((3, NX, NY, NZ), F32),
            pltpu.VMEM((8, 23, 8, NZ), F32),
            pltpu.VMEM((4 * (NX - 2), 23, 8, NZ), F32),
            pltpu.VMEM((NX, NY, NZ), jnp.int32),
            pltpu.VMEM((FACE, RACKS), jnp.int32),
            pltpu.VMEM((FACE, RACKS), jnp.int32),
            pltpu.VMEM((slabs, 128), jnp.int32),
            pltpu.VMEM((KINDS, 128, 256), BF16),
            pltpu.VMEM((KINDS, tiles * 128), F32),
            pltpu.VMEM((KINDS, tiles * 128), F32),
            pltpu.VMEM((RACKS, tiles * 128), BF16),
            pltpu.VMEM((3, 2, 5, NY, NZ), BF16),
            pltpu.VMEM((3, 2, 5, NY, NZ), BF16),
            pltpu.VMEM((3, 2, 5, NX, NZ), BF16),
            pltpu.VMEM((3, 2, 5, NX, NZ), BF16),
            pltpu.VMEM((3, 4, 8, NZ), F32),
            pltpu.VMEM((3, 2, NX, NZ), F32),
            pltpu.VMEM((3, 2, NX, NZ), F32),
            pltpu.VMEM((slabs, RACKS, 128), BF16),
            pltpu.VMEM((2, slabs, RACKS, 128), BF16),
            pltpu.VMEM((slabs * RACKS, 128), jnp.int32),
            pltpu.VMEM((NX * NY, RACKS), BF16),
            pltpu.VMEM((NZ, RACKS), BF16),
            pltpu.VMEM((NX * NY, RACKS), BF16),
            pltpu.VMEM((NZ, RACKS), BF16),
            pltpu.VMEM((RACKS, 128), F32),
            pltpu.VMEM((2, RACKS, 128), F32),
            pltpu.VMEM((8, 128), F32),
            pltpu.VMEM((slabs, RACKS, 128), F32),
            pltpu.VMEM((slabs // 2 - 1, 2, RACKS, 128), F32),
            pltpu.VMEM((2, RACKS, 128), F32),
            pltpu.VMEM((RACKS, 128), F32),
            pltpu.VMEM((8, 128), F32),
            pltpu.VMEM((tiles, 8, 128), F32),
            pltpu.VMEM((8, 128), F32),
            pltpu.VMEM((tiles, 8, 128), F32),
            dma((NX,)),
            dma((1,)),
            dma((8,)),
            dma((3, 2)),
            dma((3, 2)),
            dma((3, 2)),
            dma((3, 2)),
            dma((3, 4)),
            dma((3, 4)),
            dma((3, 4)),
            dma((3, 4)),
            dma((slabs,)),
            dma((slabs,)),
            dma((3,)),
            dma((3,)),
            dma((1,)),
            dma((1,)),
            dma((2,)),
            dma((2,)),
        ],
        compiler_params=pltpu.CompilerParams(
            collective_id=0, has_side_effects=True, vmem_limit_bytes=46 * 1024 * 1024
        ),
    )(*(pltpu.with_memory_space_constraint(a, pltpu.HBM) for a in operands))
    return pl.pallas_call(
        flush,
        out_shape=tuple(jax.ShapeDtypeStruct(shape, F32) for shape in results),
        in_specs=[vmem] * 3,
        out_specs=(hbm,) * 3,
        scratch_shapes=[dma((21,))],
        compiler_params=pltpu.CompilerParams(vmem_limit_bytes=1024 * 1024),
    )(*outs)


def solution(mesh):
    slabs, tiles = mesh.shape["slab"], mesh.shape["tile"]
    return jax.shard_map(
        functools.partial(per_device, slabs, tiles),
        mesh=mesh,
        in_specs=(
            P(None, "slab", "tile", None),
            P("slab", "tile", None),
            P("slab", "tile", None),
            P(),
            P(),
            P(),
            P(None, "tile", "slab"),
            P(),
            P(),
            P("slab", None),
        ),
        out_specs=(P(None, "slab", "tile", None), P("slab", "tile", None), P("slab", "tile")),
        check_vma=False,
    )
```
